32 devices in a mesh: rep: 2 (over y), frame: 16 (over z, x, core).
Axes of the slice: x: 2, y: 2, z: 4, core: 2. Of those that a mesh axis runs over, the one named last changes fastest.
Arguments:
- frames: bfloat16 [4096, 512], P(('rep', 'frame')), parts along dimension 0, may hold values from -6 to 6
- segment: int32 [4096], P(('rep', 'frame')), parts along dimension 0, may hold values from 0 to 8, as said below
- latents: bfloat16 [2048, 1024], P('frame'), may hold values from -1.5 to 1.5
- latent_queries: bfloat16 [2048, 1024], P('frame'), may hold values from -240 to 240
- w_kv: bfloat16 [512, 2048], replicated, may hold values from -0.25 to 0.25
- w_cross_out: bfloat16 [1024, 1024], replicated, may hold values from -0.1875 to 0.1875
- w_self_qkv: bfloat16 [1024, 3072], replicated
- w_self_out: bfloat16 [1024, 1024], replicated, may hold values from -0.1875 to 0.1875
Outputs:
- encoded: bfloat16 [4096, 1024], P(('rep', 'frame')), parts along dimension 0
The draws below stay inside these ranges and needn't reach their ends.
There are 2 independent parts, one for each index of `rep`. The reference program is written for one: setup_inputs(seed, part) draws one part's arguments, and reference() takes and returns one part's arrays. A program takes and returns all parts, laid end to end along the dimension named above; an argument that names none is the same for every part. Nothing has to cross between parts.
Inputs may be any that keep to these rules, and one draw needn't show every extreme that they name: `segment`: ids are constant over aligned runs of 64 frames; 0 marks silence; every id from 1 to 8 labels some frame; the share of silent frames differs between regions of the recording.
All inputs are finite; a program needn't handle non-finite values.
Results may differ from the reference program's by a relative error of at most 0.014.
The reference program's roundings to bfloat16 on the way (of `normed`, `keyval`, `cross`, `triple`, `probs` and `attended`) count: a program that leaves them out, or rounds other values in their place, can miss the bound.
Values may be sent and summed in bfloat16 or wider, within the bound.
No kernel may reach another device: no remote copies, remote signals or barrier semaphores. Data moves between devices by JAX's collectives and lax.ppermute only.
A program may use at most 128 MiB of HBM per device.

```python
import math
import jax
import jax.numpy as jnp
from jax import lax

D = 1024
C_IN = 512
H = 16
HEAD_DIM = 64
L = 2048
NB = 8
RUN = 64
F_DEV = 128
FRAMES = 2048
N_FRAME = 16


def draw_latent_queries(key, part):
    base = jax.random.truncated_normal(jax.random.fold_in(key, 3), -4.0, 4.0, (L, D), jnp.float32) * 2.5
    return base.astype(jnp.bfloat16)


def draw_w_self_qkv(key, part):
    rest = jax.random.truncated_normal(jax.random.fold_in(key, 7), -4.0, 4.0, (D, 2 * D), jnp.float32) / math.sqrt(D)
    fresh = jax.random.truncated_normal(jax.random.fold_in(key, 5), -4.0, 4.0, (D, D), jnp.float32)
    front = fresh * (2.5 / math.sqrt(D))
    return jnp.concatenate([front, rest], axis=1).astype(jnp.bfloat16)


def draw_segment(key, part):
    runs = FRAMES // RUN
    region = jnp.arange(runs, dtype=jnp.int32) * 8 // runs
    rates = jax.random.randint(jax.random.fold_in(key, 21), (8,), 1, 10)
    silent = jax.random.randint(jax.random.fold_in(key, 22), (runs,), 0, 10) < rates[region]
    label = jax.random.randint(jax.random.fold_in(key, 23), (runs,), 1, NB + 1).astype(jnp.int32)
    label = jnp.where(silent, jnp.int32(0), label)
    order = jax.random.permutation(jax.random.fold_in(key, 24), runs)
    label = label.at[order[:NB]].set(jnp.arange(1, NB + 1, dtype=jnp.int32))
    return jnp.repeat(label, RUN, total_repeat_length=FRAMES).astype(jnp.int32)


def level_of(key, shape, split, smallest, largest):
    gain, own = 1.0, jax.random.fold_in(key, 6)
    for position, shards_of in split:
        heights = jnp.exp(jax.random.uniform(jax.random.fold_in(own, position), (shards_of,), jnp.float32, smallest / len(split), largest / len(split)))
        gain = gain * jnp.repeat(heights, shape[position] // shards_of).reshape([-1 if axis == position else 1 for axis in range(len(shape))])
    return gain


def centred(key, extent, scale, limit, split=(), held_as=jnp.bfloat16):
    result = scale * jax.random.normal(key, extent, jnp.float32)
    if split:
        result = result * level_of(key, extent, split, -0.22, 0.18)
    return jnp.clip(result, -limit, limit).astype(held_as)


def setup_inputs(seed: int = 0, part: int = 0) -> dict:
    keys = jax.random.split(jax.random.key(seed), 9)
    part_keys = jax.random.split(jax.random.fold_in(keys[8], part), 9)
    frames = centred(part_keys[0], (FRAMES, C_IN), 1.0, 6.0, ((0, 16),))
    segment = draw_segment(jax.random.fold_in(jax.random.fold_in(keys[8], part), 71), part)
    latents = centred(keys[2], (L, D), 0.25, 1.5, ((0, 16),))
    latent_queries = draw_latent_queries(jax.random.fold_in(keys[8], 71), part)
    w_kv = centred(keys[4], (C_IN, 2 * D), C_IN ** -0.5, 0.25)
    w_cross_out = centred(keys[5], (D, D), D ** -0.5, 0.1875)
    w_self_qkv = draw_w_self_qkv(jax.random.fold_in(keys[8], 71), part)
    w_self_out = centred(keys[7], (D, D), D ** -0.5, 0.1875)
    return {"frames": frames, "segment": segment, "latents": latents, "latent_queries": latent_queries, "w_kv": w_kv, "w_cross_out": w_cross_out, "w_self_qkv": w_self_qkv, "w_self_out": w_self_out}


NEG = -1e+30

def layer_norm(inputs):
    centre = inputs - lax.optimization_barrier(jnp.mean(inputs, axis=-1, keepdims=True))
    spread = lax.optimization_barrier(jnp.mean(centre * centre, axis=-1, keepdims=True))
    return centre * lax.rsqrt(spread + 1e-05)

def reference(frames, segment, latents, latent_queries, w_kv, w_cross_out, w_self_qkv, w_self_out):
    scale = 1.0 / math.sqrt(HEAD_DIM)
    normed = layer_norm(frames.astype(jnp.float32)).astype(jnp.bfloat16)
    keyval = jnp.dot(normed, w_kv, preferred_element_type=jnp.float32).astype(jnp.bfloat16)
    key_blocks = keyval[:, :D].reshape(N_FRAME, F_DEV, H, HEAD_DIM)
    value_blocks = keyval[:, D:].reshape(N_FRAME, F_DEV, H, HEAD_DIM)
    label_blocks = segment.reshape(N_FRAME, F_DEV)
    latent_full = latents.astype(jnp.float32)
    query_heads = latent_queries.reshape(L, H, HEAD_DIM).astype(jnp.float32)
    wanted = (jnp.arange(L, dtype=jnp.int32) // (L // NB) + 1).astype(jnp.int32)

    def fold_block(carry, item):
        run_max, run_total, run_acc = carry
        key_blk, value_blk, label_blk = item
        allowed = (label_blk[None, :] == wanted[:, None])[:, None, :]
        score = jnp.einsum('lhe,fhe->lhf', query_heads, key_blk.astype(jnp.float32)) * scale
        score = jnp.where(allowed, score, NEG)
        block_max = lax.optimization_barrier(jnp.max(score, axis=2))
        weights = jnp.where(allowed, jnp.exp(score - block_max[:, :, None]), 0.0)
        block_total = lax.optimization_barrier(jnp.sum(weights, axis=2))
        rounded = lax.optimization_barrier(weights.astype(jnp.bfloat16))
        block_acc = jnp.einsum('lhf,fhe->lhe', rounded.astype(jnp.float32), value_blk.astype(jnp.float32))
        new_max = jnp.maximum(run_max, block_max)
        old_factor = jnp.exp(run_max - new_max)
        new_factor = jnp.exp(block_max - new_max)
        run_total = run_total * old_factor + block_total * new_factor
        run_acc = run_acc * old_factor[:, :, None] + block_acc * new_factor[:, :, None]
        return ((new_max, run_total, run_acc), None)
    start = (jnp.full((L, H), NEG, jnp.float32), jnp.zeros((L, H), jnp.float32), jnp.zeros((L, H, HEAD_DIM), jnp.float32))
    (run_max, run_total, run_acc), _ = lax.scan(fold_block, start, (key_blocks, value_blocks, label_blocks))
    cross = (run_acc / run_total[:, :, None]).reshape(L, D).astype(jnp.bfloat16)
    mixed = latent_full + jnp.dot(cross, w_cross_out, preferred_element_type=jnp.float32)
    normed_latent = layer_norm(mixed).astype(jnp.bfloat16)
    triple = jnp.dot(normed_latent, w_self_qkv, preferred_element_type=jnp.float32).astype(jnp.bfloat16)
    self_query = triple[:, :D].reshape(L, H, HEAD_DIM).astype(jnp.float32)
    self_key = triple[:, D:2 * D].reshape(L, H, HEAD_DIM).astype(jnp.float32)
    self_value = triple[:, 2 * D:].reshape(L, H, HEAD_DIM).astype(jnp.float32)
    score = jnp.einsum('lhe,mhe->hlm', self_query, self_key) * scale
    peak = lax.optimization_barrier(jnp.max(score, axis=2, keepdims=True))
    expo = jnp.exp(score - peak)
    probs = lax.optimization_barrier((expo / lax.optimization_barrier(jnp.sum(expo, axis=2, keepdims=True))).astype(jnp.bfloat16))
    attended = jnp.einsum('hlm,mhe->lhe', probs.astype(jnp.float32), self_value)
    attended = attended.reshape(L, D).astype(jnp.bfloat16)
    return (mixed + jnp.dot(attended, w_self_out, preferred_element_type=jnp.float32)).astype(jnp.bfloat16)
```

```python
import functools
import math

import jax
import jax.numpy as jnp
from jax import lax
from jax.experimental import pallas as pl
from jax.experimental.pallas import tpu as pltpu
from jax.sharding import PartitionSpec as P

H = 16
HEAD_DIM = 64
L = 2048
NB = 8


NEG = -1e30


def layer_norm(inputs):
    centre = inputs - jnp.mean(inputs, axis=-1, keepdims=True)
    spread = jnp.mean(centre * centre, axis=-1, keepdims=True)
    return centre * lax.rsqrt(spread + 1e-05)


def shards_any(frames, segment, latents, latent_queries, w_kv, w_cross_out, w_self_qkv, w_self_out):
    feature_width = w_kv.shape[1] // 2
    owned_rows = latents.shape[0]
    frame_count = frames.shape[0]
    scale = 1.0 / math.sqrt(HEAD_DIM)
    block_rows = L // NB
    latent_full = latents.astype(jnp.float32)
    normed = layer_norm(frames.astype(jnp.float32)).astype(jnp.bfloat16)
    keyval = jnp.dot(normed, w_kv, preferred_element_type=jnp.float32).astype(jnp.bfloat16)
    key_heads = keyval[:, :feature_width].reshape(frame_count, H, HEAD_DIM).transpose(1, 0, 2)
    value_heads = keyval[:, feature_width:].reshape(frame_count, H, HEAD_DIM).transpose(1, 0, 2)
    total_rows = owned_rows * lax.axis_size("frame")
    piece = lax.all_gather(latent_queries, "frame", axis=0, tiled=True)
    piece_rows = piece.shape[0]
    block_ids = jnp.arange(piece_rows, dtype=jnp.int32) // block_rows + 1
    allowed = segment[None, :] == block_ids[:, None]
    query_heads = piece.reshape(piece_rows, H, HEAD_DIM).transpose(1, 0, 2)

    def one_head(item):
        query_head, key_head, value_head = item
        score = (
            jnp.einsum("re,fe->rf", query_head, key_head, preferred_element_type=jnp.float32)
            * scale
        )
        score = jnp.where(allowed, score, NEG)
        block_max = jnp.max(score, axis=1)
        weights = jnp.where(allowed, jnp.exp(score - block_max[:, None]), 0.0)
        block_total = jnp.sum(weights, axis=1)
        summed = jnp.dot(
            weights.astype(jnp.bfloat16), value_head, preferred_element_type=jnp.float32
        )
        return (block_max, block_total, summed)

    block_max, block_total, summed = lax.map(one_head, (query_heads, key_heads, value_heads))
    run_max = block_max.T
    run_total = block_total.T
    joined = summed.transpose(1, 0, 2).reshape(piece_rows, feature_width)
    run_acc = joined
    run_max, run_total, run_acc = (run_max, run_total, run_acc)
    sources = lax.axis_size("frame")
    got_acc, got_max, got_total = (
        lax.all_to_all(
            run_acc.reshape(sources, owned_rows, feature_width),
            "frame",
            split_axis=0,
            concat_axis=0,
            tiled=True,
        ),
        lax.all_to_all(
            run_max.reshape(sources, owned_rows, H),
            "frame",
            split_axis=0,
            concat_axis=0,
            tiled=True,
        ),
        lax.all_to_all(
            run_total.reshape(sources, owned_rows, H),
            "frame",
            split_axis=0,
            concat_axis=0,
            tiled=True,
        ),
    )
    global_max = jnp.max(got_max, axis=0)
    factor = jnp.exp(got_max - global_max[None])
    norms = jnp.sum(got_total * factor, axis=0)
    sums = jnp.sum(
        got_acc.reshape(sources, owned_rows, H, HEAD_DIM) * factor[:, :, :, None], axis=0
    )
    cross = (sums / norms[:, :, None]).reshape(owned_rows, feature_width)
    cross = cross.astype(jnp.bfloat16)
    mixed = latent_full + jnp.dot(cross, w_cross_out, preferred_element_type=jnp.float32)
    normed_latent = layer_norm(mixed).astype(jnp.bfloat16)
    triple = jnp.dot(normed_latent, w_self_qkv, preferred_element_type=jnp.float32).astype(
        jnp.bfloat16
    )
    self_query = triple[:, :feature_width].reshape(owned_rows, H, HEAD_DIM)
    self_key = triple[:, feature_width : 2 * feature_width]
    self_value = triple[:, 2 * feature_width :]
    every_key, every_value = (
        lax.all_gather(self_key, "frame", axis=0, tiled=True),
        lax.all_gather(self_value, "frame", axis=0, tiled=True),
    )
    every_key = every_key.reshape(total_rows, H, HEAD_DIM)
    every_value = every_value.reshape(total_rows, H, HEAD_DIM)
    score = (
        jnp.einsum("rhe,mhe->hrm", self_query, every_key, preferred_element_type=jnp.float32)
        * scale
    )
    peak = jnp.max(score, axis=2, keepdims=True)
    expo = jnp.exp(score - peak)
    probs = (expo / jnp.sum(expo, axis=2, keepdims=True)).astype(jnp.bfloat16)
    attended = jnp.einsum("hrm,mhe->rhe", probs, every_value, preferred_element_type=jnp.float32)
    attended = attended.reshape(owned_rows, feature_width).astype(jnp.bfloat16)
    return (mixed + jnp.dot(attended, w_self_out, preferred_element_type=jnp.float32)).astype(
        jnp.bfloat16
    )


RUN = 64
PAD = 8
GROUP = 4
WIDE = 256
PER = WIDE // HEAD_DIM
BF16 = jnp.bfloat16
F32 = jnp.float32
VMEM = pltpu.VMEM


def head_stack(block):
    lane = lax.broadcasted_iota(jnp.int32, block.shape, 1) // HEAD_DIM
    return jnp.concatenate([jnp.where(lane == h, block, 0.0) for h in range(PER)], axis=0)


def head_pick(tall, rows):
    lane = lax.broadcasted_iota(jnp.int32, (rows, WIDE), 1) // HEAD_DIM
    out = jnp.broadcast_to(tall[:rows], (rows, WIDE))
    for h in range(1, PER):
        out = jnp.where(lane == h, jnp.broadcast_to(tall[h * rows : (h + 1) * rows], (rows, WIDE)), out)
    return out


def attend(stack, keys, values, valid, state, rows):
    score = lax.dot_general(stack, keys, (((1,), (1,)), ((), ())), preferred_element_type=F32)
    if valid is not None:
        score = jnp.where(valid, score, NEG)
    top = jnp.max(score, axis=1, keepdims=True)
    if state is not None:
        old_top, old_total, old_acc = state
        top = jnp.maximum(top, old_top)
    weights = jnp.exp(score - top)
    if valid is not None:
        weights = jnp.where(valid, weights, 0.0)
    total = jnp.sum(weights, axis=1, keepdims=True)
    acc = head_pick(jnp.dot(weights.astype(BF16), values, preferred_element_type=F32), rows)
    if state is not None:
        fade = jnp.exp(old_top - top)
        total = total + old_total * fade
        acc = acc + old_acc * head_pick(fade, rows)
    return top, total, acc


def norm(v):
    centre = v - jnp.mean(v, axis=-1, keepdims=True)
    spread = jnp.mean(centre * centre, axis=-1, keepdims=True)
    return centre * lax.rsqrt(spread + 1e-05)


def cross_kernel(n_pieces, *refs):
    pieces = refs[:n_pieces]
    (latents, queries, w_kv, w_out, mixed_out, normed_out,
     picked, stacks, tops, totals, accs, joined, count) = refs[n_pieces:]
    rows, width = latents.shape
    scale = 1.0 / math.sqrt(HEAD_DIM)
    mine = (lax.axis_index("frame") * rows) // (L // NB) + 1
    ids = [
        [jnp.max(piece[run, RUN : RUN + PAD, :128].astype(F32)).astype(jnp.int32) for run in range(piece.shape[0])]
        for piece in pieces
    ]
    count[0] = 0
    for piece, labels in zip(pieces, ids):
        for run, label in enumerate(labels):
            @pl.when(label == mine)
            def _(piece=piece, run=run):
                at = count[0]
                picked[at] = piece[run, :RUN, :]
                count[0] = at + 1
    found = count[0]
    for extra in range(GROUP - 1):
        picked[found + extra] = jnp.zeros(picked.shape[1:], BF16)
    for j in range(width // WIDE):
        block = queries[:, j * WIDE : (j + 1) * WIDE].astype(F32) * scale
        stacks[j] = head_stack(block).astype(BF16)
    tops[...] = jnp.full(tops.shape, NEG, F32)
    totals[...] = jnp.zeros(totals.shape, F32)
    accs[...] = jnp.zeros(accs.shape, F32)

    def one_group(g, carry):
        frames = picked[pl.ds(g * GROUP, GROUP)].reshape(GROUP * RUN, picked.shape[2])
        normed = norm(frames.astype(F32)).astype(BF16)
        left = (found - g * GROUP) * RUN
        valid = lax.broadcasted_iota(jnp.int32, (PER * rows, GROUP * RUN), 1) < left
        for j in range(width // WIDE):
            cols = slice(j * WIDE, (j + 1) * WIDE)
            keys = jnp.dot(normed, w_kv[:, j * WIDE : (j + 1) * WIDE], preferred_element_type=F32).astype(BF16)
            values = jnp.dot(
                normed, w_kv[:, width + j * WIDE : width + (j + 1) * WIDE], preferred_element_type=F32
            ).astype(BF16)
            tops[j], totals[j], accs[:, cols] = attend(
                stacks[j], keys, values, valid, (tops[j], totals[j], accs[:, cols]), rows
            )
        return carry

    lax.fori_loop(0, (found + GROUP - 1) // GROUP, one_group, 0)
    for j in range(width // WIDE):
        cols = slice(j * WIDE, (j + 1) * WIDE)
        joined[:, cols] = (accs[:, cols] / head_pick(totals[j], rows)).astype(BF16)
    mixed = latents[...].astype(F32) + jnp.dot(joined[...], w_out[...], preferred_element_type=F32)
    mixed_out[...] = mixed
    normed_out[...] = norm(mixed).astype(BF16)


def project_attend(sources, w_qkv, stacks, state, width, rows):
    normed = jnp.concatenate([s[...] for s in sources], axis=0) if len(sources) > 1 else sources[0][...]
    out = []
    for j in range(width // WIDE):
        keys = jnp.dot(normed, w_qkv[:, width + j * WIDE : width + (j + 1) * WIDE], preferred_element_type=F32)
        values = jnp.dot(
            normed, w_qkv[:, 2 * width + j * WIDE : 2 * width + (j + 1) * WIDE], preferred_element_type=F32
        )
        out.append(attend(stacks(j), keys.astype(BF16), values.astype(BF16), None, state(j), rows))
    return out


def first_kernel(normed, w_qkv, stacks, tops, totals, accs):
    rows, width = normed.shape
    scale = 1.0 / math.sqrt(HEAD_DIM)
    for j in range(width // WIDE):
        query = jnp.dot(normed[...], w_qkv[:, j * WIDE : (j + 1) * WIDE], preferred_element_type=F32).astype(BF16)
        stacks[j] = head_stack(query.astype(F32) * scale).astype(BF16)
    found = project_attend([normed], w_qkv, lambda j: stacks[j], lambda j: None, width, rows)
    for j, (top, total, acc) in enumerate(found):
        tops[j], totals[j], accs[:, j * WIDE : (j + 1) * WIDE] = top, total, acc


def next_kernel(n_pieces, *refs):
    sources = refs[:n_pieces]
    w_qkv, stacks, tops_in, totals_in, accs_in, tops, totals, accs = refs[n_pieces:]
    rows, width = accs.shape
    for j in range(width // WIDE):
        cols = slice(j * WIDE, (j + 1) * WIDE)
    found = project_attend(
        sources, w_qkv, lambda j: stacks[j],
        lambda j: (tops_in[j], totals_in[j], accs_in[:, j * WIDE : (j + 1) * WIDE]), width, rows,
    )
    for j, (top, total, acc) in enumerate(found):
        tops[j], totals[j], accs[:, j * WIDE : (j + 1) * WIDE] = top, total, acc


def last_kernel(n_pieces, *refs):
    sources = refs[:n_pieces]
    w_qkv, stacks, tops_in, totals_in, accs_in, mixed, w_out, out, joined = refs[n_pieces:]
    rows, width = accs_in.shape
    found = project_attend(
        sources, w_qkv, lambda j: stacks[j],
        lambda j: (tops_in[j], totals_in[j], accs_in[:, j * WIDE : (j + 1) * WIDE]), width, rows,
    )
    for j, (top, total, acc) in enumerate(found):
        joined[:, j * WIDE : (j + 1) * WIDE] = (acc / head_pick(total, rows)).astype(BF16)
    out[...] = (mixed[...] + jnp.dot(joined[...], w_out[...], preferred_element_type=F32)).astype(BF16)


def on_chip(x):
    return pltpu.with_memory_space_constraint(x, VMEM)


def call(kernel, args, outs, scratch, name, flops, limit, aliases=None):
    return pl.pallas_call(
        kernel,
        out_shape=outs,
        in_specs=[pl.BlockSpec(memory_space=VMEM)] * len(args),
        out_specs=jax.tree.map(lambda _: pl.BlockSpec(memory_space=VMEM), outs, is_leaf=lambda o: hasattr(o, "shape")),
        scratch_shapes=scratch,
        compiler_params=pltpu.CompilerParams(vmem_limit_bytes=limit << 20),
        cost_estimate=pl.CostEstimate(flops=flops, bytes_accessed=1 << 20, transcendentals=0),
        input_output_aliases=aliases or {},
        name=name,
    )(*[on_chip(a) for a in args])


def shards_ring(frames, segment, latents, latent_queries, w_kv, w_cross_out, w_self_qkv, w_self_out):
    chips = lax.axis_size("frame") // 2
    rows, width = latents.shape
    order = [2 * k for k in range(chips // 2)] + [2 * k + 1 for k in reversed(range(chips // 2))]
    swap = [(i, i ^ 1) for i in range(2 * chips)]
    ring = []
    for at in range(chips):
        here, there = order[at], order[(at + 1) % chips]
        ring += [(2 * here, 2 * there), (2 * there + 1, 2 * here + 1)]

    def go(x):
        return lax.ppermute(x, "frame", ring)

    def cross_over(x):
        return lax.ppermute(x, "frame", swap)

    def hops(x):
        near, far = x, cross_over(x)
        found = [[near], [far]]
        for hop in range(1, chips // 2):
            near, far = go(near), go(far)
            found += [[near, far], [cross_over(near), cross_over(far)]]
        near = go(near)
        return found + [[near, cross_over(near)]]

    runs = frames.shape[0] // RUN
    tag = jnp.broadcast_to(segment.reshape(runs, RUN)[:, :1, None].astype(BF16), (runs, PAD, frames.shape[1]))
    tagged = jnp.concatenate([frames.reshape(runs, RUN, frames.shape[1]), tag], axis=1)
    pieces = [piece for group in hops(tagged) for piece in group]
    groups = width // WIDE
    tall = PER * rows
    all_runs = len(pieces) * runs
    state = (VMEM((groups, tall, 1), F32), VMEM((groups, tall, 1), F32), VMEM((rows, width), F32))
    mixed, normed = call(
        functools.partial(cross_kernel, len(pieces)),
        pieces + [latents, latent_queries, w_kv, w_cross_out],
        (VMEM((rows, width), F32), VMEM((rows, width), BF16)),
        [
            VMEM((all_runs + GROUP, RUN, frames.shape[1]), BF16),
            VMEM((groups, tall, WIDE), BF16),
            *state,
            VMEM((rows, width), BF16),
            pltpu.SMEM((1,), jnp.int32),
        ],
        "cross", 4 << 30, 16,
    )
    arrivals = hops(normed)
    stacks, tops, totals, accs = call(
        first_kernel, [normed, w_self_qkv],
        (VMEM((groups, tall, WIDE), BF16), *state), [], "first", 1 << 30, 12,
    )
    for sources in arrivals[1:-1]:
        n = len(sources)
        tops, totals, accs = call(
            functools.partial(next_kernel, n), sources + [w_self_qkv, stacks, tops, totals, accs],
            state, [], "next", n << 29, 12, {n + 2: 0, n + 3: 1, n + 4: 2},
        )
    sources = arrivals[-1]
    return call(
        functools.partial(last_kernel, len(sources)),
        sources + [w_self_qkv, stacks, tops, totals, accs, mixed, w_self_out],
        jax.ShapeDtypeStruct((rows, width), BF16),
        [VMEM((rows, width), BF16)], "last", 1 << 30, 12,
    )


def solution(mesh):
    placed = (
        P(("rep", "frame"), None),
        P(("rep", "frame")),
        P("frame", None),
        P("frame", None),
        P(),
        P(),
        P(),
        P(),
    )
    step = shards_ring if mesh.shape["frame"] == 16 else shards_any
    return jax.shard_map(
        step, mesh=mesh, in_specs=placed, out_specs=P(("rep", "frame"), None), check_vma=False
    )
```

```python
import functools
import math

import jax
import jax.numpy as jnp
from jax import lax
from jax.experimental import pallas as pl
from jax.experimental.pallas import tpu as pltpu
from jax.sharding import PartitionSpec as P

H = 16
HEAD_DIM = 64
L = 2048
NB = 8


NEG = -1e30


def layer_norm(inputs):
    centre = inputs - jnp.mean(inputs, axis=-1, keepdims=True)
    spread = jnp.mean(centre * centre, axis=-1, keepdims=True)
    return centre * lax.rsqrt(spread + 1e-05)


def shards_any(frames, segment, latents, latent_queries, w_kv, w_cross_out, w_self_qkv, w_self_out):
    feature_width = w_kv.shape[1] // 2
    owned_rows = latents.shape[0]
    frame_count = frames.shape[0]
    scale = 1.0 / math.sqrt(HEAD_DIM)
    block_rows = L // NB
    latent_full = latents.astype(jnp.float32)
    normed = layer_norm(frames.astype(jnp.float32)).astype(jnp.bfloat16)
    keyval = jnp.dot(normed, w_kv, preferred_element_type=jnp.float32).astype(jnp.bfloat16)
    key_heads = keyval[:, :feature_width].reshape(frame_count, H, HEAD_DIM).transpose(1, 0, 2)
    value_heads = keyval[:, feature_width:].reshape(frame_count, H, HEAD_DIM).transpose(1, 0, 2)
    total_rows = owned_rows * lax.axis_size("frame")
    piece = lax.all_gather(latent_queries, "frame", axis=0, tiled=True)
    piece_rows = piece.shape[0]
    block_ids = jnp.arange(piece_rows, dtype=jnp.int32) // block_rows + 1
    allowed = segment[None, :] == block_ids[:, None]
    query_heads = piece.reshape(piece_rows, H, HEAD_DIM).transpose(1, 0, 2)

    def one_head(item):
        query_head, key_head, value_head = item
        score = (
            jnp.einsum("re,fe->rf", query_head, key_head, preferred_element_type=jnp.float32)
            * scale
        )
        score = jnp.where(allowed, score, NEG)
        block_max = jnp.max(score, axis=1)
        weights = jnp.where(allowed, jnp.exp(score - block_max[:, None]), 0.0)
        block_total = jnp.sum(weights, axis=1)
        summed = jnp.dot(
            weights.astype(jnp.bfloat16), value_head, preferred_element_type=jnp.float32
        )
        return (block_max, block_total, summed)

    block_max, block_total, summed = lax.map(one_head, (query_heads, key_heads, value_heads))
    run_max = block_max.T
    run_total = block_total.T
    joined = summed.transpose(1, 0, 2).reshape(piece_rows, feature_width)
    run_acc = joined
    run_max, run_total, run_acc = (run_max, run_total, run_acc)
    sources = lax.axis_size("frame")
    got_acc, got_max, got_total = (
        lax.all_to_all(
            run_acc.reshape(sources, owned_rows, feature_width),
            "frame",
            split_axis=0,
            concat_axis=0,
            tiled=True,
        ),
        lax.all_to_all(
            run_max.reshape(sources, owned_rows, H),
            "frame",
            split_axis=0,
            concat_axis=0,
            tiled=True,
        ),
        lax.all_to_all(
            run_total.reshape(sources, owned_rows, H),
            "frame",
            split_axis=0,
            concat_axis=0,
            tiled=True,
        ),
    )
    global_max = jnp.max(got_max, axis=0)
    factor = jnp.exp(got_max - global_max[None])
    norms = jnp.sum(got_total * factor, axis=0)
    sums = jnp.sum(
        got_acc.reshape(sources, owned_rows, H, HEAD_DIM) * factor[:, :, :, None], axis=0
    )
    cross = (sums / norms[:, :, None]).reshape(owned_rows, feature_width)
    cross = cross.astype(jnp.bfloat16)
    mixed = latent_full + jnp.dot(cross, w_cross_out, preferred_element_type=jnp.float32)
    normed_latent = layer_norm(mixed).astype(jnp.bfloat16)
    triple = jnp.dot(normed_latent, w_self_qkv, preferred_element_type=jnp.float32).astype(
        jnp.bfloat16
    )
    self_query = triple[:, :feature_width].reshape(owned_rows, H, HEAD_DIM)
    self_key = triple[:, feature_width : 2 * feature_width]
    self_value = triple[:, 2 * feature_width :]
    every_key, every_value = (
        lax.all_gather(self_key, "frame", axis=0, tiled=True),
        lax.all_gather(self_value, "frame", axis=0, tiled=True),
    )
    every_key = every_key.reshape(total_rows, H, HEAD_DIM)
    every_value = every_value.reshape(total_rows, H, HEAD_DIM)
    score = (
        jnp.einsum("rhe,mhe->hrm", self_query, every_key, preferred_element_type=jnp.float32)
        * scale
    )
    peak = jnp.max(score, axis=2, keepdims=True)
    expo = jnp.exp(score - peak)
    probs = (expo / jnp.sum(expo, axis=2, keepdims=True)).astype(jnp.bfloat16)
    attended = jnp.einsum("hrm,mhe->rhe", probs, every_value, preferred_element_type=jnp.float32)
    attended = attended.reshape(owned_rows, feature_width).astype(jnp.bfloat16)
    return (mixed + jnp.dot(attended, w_self_out, preferred_element_type=jnp.float32)).astype(
        jnp.bfloat16
    )


RUN = 64
PAD = 8
GROUP = 4
WIDE = 256
PAIR = 2 * HEAD_DIM
BF16 = jnp.bfloat16
F32 = jnp.float32
VMEM = pltpu.VMEM


def norm(v):
    centre = v - jnp.mean(v, axis=-1, keepdims=True)
    spread = jnp.mean(centre * centre, axis=-1, keepdims=True)
    return centre * lax.rsqrt(spread + 1e-05)


def fill_stacks(stacks, j, blocks):
    for q in range(WIDE // PAIR):
        i = j * (WIDE // PAIR) + q
        wide = stacks.shape[2] // 2
        at = 0
        for block in blocks:
            turned = block[:, q * PAIR : (q + 1) * PAIR].T
            n = turned.shape[1]
            none = jnp.zeros((HEAD_DIM, n), BF16)
            stacks[i, :HEAD_DIM, at : at + n] = turned[:HEAD_DIM]
            stacks[i, HEAD_DIM:, at : at + n] = none
            stacks[i, :HEAD_DIM, wide + at : wide + at + n] = none
            stacks[i, HEAD_DIM:, wide + at : wide + at + n] = turned[HEAD_DIM:]
            at += n


def project(normed, weights, at, width, keys, values):
    n = normed.shape[0]
    for j in range(width // WIDE):
        cols = slice(j * WIDE, (j + 1) * WIDE)
        k = jnp.dot(normed, weights[:, at + j * WIDE : at + (j + 1) * WIDE], preferred_element_type=F32)
        keys[:n, cols] = k.astype(BF16)
        v = jnp.dot(
            normed, weights[:, at + width + j * WIDE : at + width + (j + 1) * WIDE], preferred_element_type=F32
        )
        values[cols, :n] = v.astype(BF16).T


def attend(n, left, stacks, keys, values, scores, probs, old, new):
    pairs, wide = stacks.shape[0], stacks.shape[2]
    half = wide // 2
    tops, totals, accs = new
    masked = left is not None
    if masked:
        valid = lax.broadcasted_iota(jnp.int32, (n, wide), 0) < left
    for i in range(pairs):
        score = jnp.dot(keys[:n, i * PAIR : (i + 1) * PAIR], stacks[i], preferred_element_type=F32)
        if masked:
            score = jnp.where(valid, score, NEG)
        scores[i, :n] = score
        top = jnp.max(score, axis=0, keepdims=True)
        tops[i : i + 1] = top if old is None else jnp.maximum(old[0][i : i + 1], top)
    for i in range(pairs):
        top = tops[i : i + 1]
        weights = jnp.exp(scores[i, :n] - top)
        if masked:
            weights = jnp.where(valid, weights, 0.0)
        total = jnp.sum(weights, axis=0, keepdims=True)
        if old is not None:
            total = total + old[1][i : i + 1] * jnp.exp(old[0][i : i + 1] - top)
        totals[i : i + 1] = total
        probs[i, :n] = weights.astype(BF16)
    for i in range(pairs):
        out = jnp.dot(values[i * PAIR : (i + 1) * PAIR, :n], probs[i, :n], preferred_element_type=F32)
        if old is not None:
            fade = jnp.exp(old[0][i : i + 1] - tops[i : i + 1])
        for h in range(2):
            rows = slice(i * PAIR + h * HEAD_DIM, i * PAIR + (h + 1) * HEAD_DIM)
            cols = slice(h * half, (h + 1) * half)
            part = out[h * HEAD_DIM : (h + 1) * HEAD_DIM, cols]
            if old is not None:
                part = part + old[2][rows, :] * fade[:, cols]
            accs[rows, :] = part


def tag_kernel(segment, frames, out):
    for run in range(out.shape[0]):
        out[run, :RUN] = frames[run * RUN : (run + 1) * RUN]
        label = segment[run * RUN].astype(F32)
        out[run, RUN:] = jnp.full((PAD, frames.shape[1]), label, F32).astype(BF16)


def queries_kernel(queries, stacks):
    scale = 1.0 / math.sqrt(HEAD_DIM)
    for j in range(queries.shape[1] // WIDE):
        block = queries[:, j * WIDE : (j + 1) * WIDE].astype(F32) * scale
        fill_stacks(stacks, j, [block.astype(BF16)])


def cross_kernel(n_pieces, *refs):
    pieces = refs[:n_pieces]
    (latents, stacks, w_kv, w_out, mixed_out, normed_out,
     picked, keys, values, scores, probs, tops, totals, accs, joined, count) = refs[n_pieces:]
    rows, width = latents.shape
    mine = (lax.axis_index("frame") * rows) // (L // NB) + 1
    ids = [
        [jnp.max(piece[run, RUN : RUN + PAD, :128].astype(F32)).astype(jnp.int32) for run in range(piece.shape[0])]
        for piece in pieces
    ]
    count[0] = 0
    for piece, labels in zip(pieces, ids):
        for run, label in enumerate(labels):
            @pl.when(label == mine)
            def _(piece=piece, run=run):
                at = count[0]
                picked[at] = piece[run, :RUN, :]
                count[0] = at + 1
    found = count[0]
    for extra in range(GROUP - 1):
        picked[found + extra] = jnp.zeros(picked.shape[1:], BF16)
    tops[...] = jnp.full(tops.shape, NEG, F32)
    totals[...] = jnp.zeros(totals.shape, F32)
    accs[...] = jnp.zeros(accs.shape, F32)
    state = (tops, totals, accs)

    def one_group(g, carry):
        n = GROUP * RUN
        frames = picked[pl.ds(g * GROUP, GROUP)].reshape(n, picked.shape[2])
        normed = norm(frames.astype(F32)).astype(BF16)
        project(normed, w_kv, 0, width, keys, values)
        old = (tops[...], totals[...], accs)
        attend(n, (found - g * GROUP) * RUN, stacks, keys, values, scores, probs, old, state)
        return carry

    lax.fori_loop(0, (found + GROUP - 1) // GROUP, one_group, 0)
    finish(accs, totals, joined)
    mixed = latents[...].astype(F32) + jnp.dot(joined[...], w_out[...], preferred_element_type=F32)
    mixed_out[...] = mixed
    normed_out[...] = norm(mixed).astype(BF16)


def finish(accs, totals, joined):
    half = totals.shape[1] // 2
    for i in range(totals.shape[0]):
        parts = []
        for h in range(2):
            rows = slice(i * PAIR + h * HEAD_DIM, i * PAIR + (h + 1) * HEAD_DIM)
            parts.append(accs[rows, :] / totals[i : i + 1, h * half : (h + 1) * half])
        joined[:, i * PAIR : (i + 1) * PAIR] = jnp.concatenate(parts, axis=0).astype(BF16).T


def first_kernel(mine, other, w_qkv, stacks, tops, totals, accs, keys, values, scores, probs):
    rows, width = mine.shape
    scale = 1.0 / math.sqrt(HEAD_DIM)
    both = jnp.concatenate([mine[...], other[...]], axis=0)
    for j in range(width // WIDE):
        query = jnp.dot(both, w_qkv[:, j * WIDE : (j + 1) * WIDE], preferred_element_type=F32).astype(BF16)
        fill_stacks(stacks, j, [(query.astype(F32) * scale).astype(BF16)])
    project(mine[...], w_qkv, width, width, keys, values)
    attend(rows, None, stacks, keys, values, scores, probs, None, (tops, totals, accs))


def next_kernel(n_pieces, *refs):
    sources = refs[:n_pieces]
    (w_qkv, stacks, old_tops, old_totals, old_accs, tops, totals, accs, keys, values, scores, probs) = refs[n_pieces:]
    width = accs.shape[0]
    block = jnp.concatenate([s[...] for s in sources], axis=0)
    project(block, w_qkv, width, width, keys, values)
    old = (old_tops[...], old_totals[...], old_accs)
    attend(block.shape[0], None, stacks, keys, values, scores, probs, old, (tops, totals, accs))


def final_kernel(tops, totals, accs, far, mixed, w_out, out, joined, merged, sums):
    width, rows = far.shape[0] - 2 * 2 * tops.shape[0], far.shape[1]
    for i in range(tops.shape[0]):
        for h in range(2):
            at = 2 * i + h
            here = slice(h * 2 * rows, h * 2 * rows + rows)
            lines = slice(i * PAIR + h * HEAD_DIM, i * PAIR + (h + 1) * HEAD_DIM)
            near_top, far_top = tops[i : i + 1, here], far[width + at : width + at + 1]
            top = jnp.maximum(near_top, far_top)
            near_fade, far_fade = jnp.exp(near_top - top), jnp.exp(far_top - top)
            far_total = far[width + 2 * tops.shape[0] + at : width + 2 * tops.shape[0] + at + 1]
            sums[i : i + 1, h * rows : (h + 1) * rows] = totals[i : i + 1, here] * near_fade + far_total * far_fade
            merged[lines] = accs[lines, :rows] * near_fade + far[lines] * far_fade
    finish(merged, sums, joined)
    out[...] = (mixed[...] + jnp.dot(joined[...], w_out[...], preferred_element_type=F32)).astype(BF16)


def last_kernel(n_pieces, *refs):
    sources = refs[:n_pieces]
    (w_qkv, stacks, old_tops, old_totals, old_accs, tops, totals, accs, away,
     keys, values, scores, probs) = refs[n_pieces:]
    next_kernel(n_pieces, *sources, w_qkv, stacks, old_tops, old_totals, old_accs, tops, totals, accs,
                keys, values, scores, probs)
    width, rows = accs.shape[0], accs.shape[1] // 2
    away[:width] = accs[:, rows:]
    for i in range(tops.shape[0]):
        for h in range(2):
            there = slice(h * 2 * rows + rows, (h + 1) * 2 * rows)
            at = 2 * i + h
            away[width + at : width + at + 1] = tops[i : i + 1, there]
            at += 2 * tops.shape[0]
            away[width + at : width + at + 1] = totals[i : i + 1, there]


def on_chip(x):
    return pltpu.with_memory_space_constraint(x, VMEM)


def call(kernel, args, outs, scratch, name, flops, limit, aliases=None, scalars=0):
    specs = [pl.BlockSpec(memory_space=pltpu.SMEM)] * scalars
    specs += [pl.BlockSpec(memory_space=VMEM)] * (len(args) - scalars)
    return pl.pallas_call(
        kernel,
        out_shape=outs,
        in_specs=specs,
        out_specs=jax.tree.map(lambda _: pl.BlockSpec(memory_space=VMEM), outs, is_leaf=lambda o: hasattr(o, "shape")),
        scratch_shapes=scratch,
        compiler_params=pltpu.CompilerParams(vmem_limit_bytes=limit << 20),
        cost_estimate=pl.CostEstimate(flops=flops, bytes_accessed=1 << 20, transcendentals=0),
        input_output_aliases=aliases or {},
        name=name,
    )(*args[:scalars], *[on_chip(a) for a in args[scalars:]])


def shards_ring(frames, segment, latents, latent_queries, w_kv, w_cross_out, w_self_qkv, w_self_out):
    chips = lax.axis_size("frame") // 2
    rows, width = latents.shape
    channels = frames.shape[1]
    order = [2 * k for k in range(chips // 2)] + [2 * k + 1 for k in reversed(range(chips // 2))]
    swap = [(i, i ^ 1) for i in range(2 * chips)]
    ahead = [(2 * order[k] + c, 2 * order[(k + 1) % chips] + c) for k in range(chips) for c in range(2)]
    behind = [(there, here) for here, there in ahead]

    def cross_over(x):
        return lax.ppermute(x, "frame", swap)

    def ring(x):
        fore, aft = x, x
        found = []
        for _ in range(1, chips // 2):
            fore, aft = lax.ppermute(fore, "frame", ahead), lax.ppermute(aft, "frame", behind)
            found.append([fore, aft])
        cut = x.shape[0] // 2
        fore, aft = lax.ppermute(fore[:cut], "frame", ahead), lax.ppermute(aft[cut:], "frame", behind)
        return found + [[fore, aft]]

    runs = frames.shape[0] // RUN
    pairs = width // PAIR
    tagged = call(
        tag_kernel, [segment, frames], VMEM((runs, RUN + PAD, channels), BF16), [], "tag", 1 << 34, 2, scalars=1
    )
    stacks = call(queries_kernel, [latent_queries], VMEM((pairs, PAIR, 2 * rows), BF16), [], "queries", 1 << 28, 4)
    pieces = [tagged, cross_over(tagged)]
    for group in ring(tagged):
        pieces += group + [cross_over(piece) for piece in group]
    all_runs = sum(piece.shape[0] for piece in pieces)

    def state(queries):
        return (VMEM((pairs, 2 * queries), F32), VMEM((pairs, 2 * queries), F32), VMEM((width, queries), F32))

    def work(n, queries):
        return [
            VMEM((n, width), BF16), VMEM((width, n), BF16),
            VMEM((pairs, n, 2 * queries), F32), VMEM((pairs, n, 2 * queries), BF16),
        ]

    mixed, normed = call(
        functools.partial(cross_kernel, len(pieces)),
        pieces + [latents, stacks, w_kv, w_cross_out],
        (VMEM((rows, width), F32), VMEM((rows, width), BF16)),
        [
            VMEM((all_runs + GROUP, RUN, channels), BF16),
            *work(GROUP * RUN, rows), *state(rows),
            VMEM((rows, width), BF16),
            pltpu.SMEM((1,), jnp.int32),
        ],
        "cross", 4 << 30, 20,
    )
    arrivals = ring(normed)
    stacks, *kept = call(
        first_kernel, [normed, cross_over(normed), w_self_qkv],
        (VMEM((pairs, PAIR, 4 * rows), BF16), *state(2 * rows)), work(rows, 2 * rows), "first", 1 << 30, 16,
    )
    for sources in arrivals[:-1]:
        n = len(sources)
        kept = call(
            functools.partial(next_kernel, n), sources + [w_self_qkv, stacks, *kept],
            state(2 * rows), work(n * rows, 2 * rows), "next", n << 30, 20, {n + 2: 0, n + 3: 1, n + 4: 2},
        )
    sources = arrivals[-1]
    n = len(sources)
    *kept, away = call(
        functools.partial(last_kernel, n), sources + [w_self_qkv, stacks, *kept],
        (*state(2 * rows), VMEM((width + 4 * pairs, rows), F32)), work(rows, 2 * rows), "last", 1 << 30, 20,
        {n + 2: 0, n + 3: 1, n + 4: 2},
    )
    return call(
        final_kernel, [*kept, cross_over(away), mixed, w_self_out],
        jax.ShapeDtypeStruct((rows, width), BF16),
        [VMEM((rows, width), BF16), VMEM((width, rows), F32), VMEM((pairs, 2 * rows), F32)],
        "final", 1 << 30, 12,
    )


def solution(mesh):
    placed = (
        P(("rep", "frame"), None),
        P(("rep", "frame")),
        P("frame", None),
        P("frame", None),
        P(),
        P(),
        P(),
        P(),
    )
    step = shards_ring if mesh.shape["frame"] == 16 else shards_any
    return jax.shard_map(
        step, mesh=mesh, in_specs=placed, out_specs=P(("rep", "frame"), None), check_vma=False
    )
```

```python
import functools
import math

import jax
import jax.numpy as jnp
from jax import lax
from jax.experimental import pallas as pl
from jax.experimental.pallas import tpu as pltpu
from jax.sharding import PartitionSpec as P

H = 16
HEAD_DIM = 64
L = 2048
NB = 8


NEG = -1e30


def layer_norm(inputs):
    centre = inputs - jnp.mean(inputs, axis=-1, keepdims=True)
    spread = jnp.mean(centre * centre, axis=-1, keepdims=True)
    return centre * lax.rsqrt(spread + 1e-05)


def shards_any(frames, segment, latents, latent_queries, w_kv, w_cross_out, w_self_qkv, w_self_out):
    feature_width = w_kv.shape[1] // 2
    owned_rows = latents.shape[0]
    frame_count = frames.shape[0]
    scale = 1.0 / math.sqrt(HEAD_DIM)
    block_rows = L // NB
    latent_full = latents.astype(jnp.float32)
    normed = layer_norm(frames.astype(jnp.float32)).astype(jnp.bfloat16)
    keyval = jnp.dot(normed, w_kv, preferred_element_type=jnp.float32).astype(jnp.bfloat16)
    key_heads = keyval[:, :feature_width].reshape(frame_count, H, HEAD_DIM).transpose(1, 0, 2)
    value_heads = keyval[:, feature_width:].reshape(frame_count, H, HEAD_DIM).transpose(1, 0, 2)
    total_rows = owned_rows * lax.axis_size("frame")
    piece = lax.all_gather(latent_queries, "frame", axis=0, tiled=True)
    piece_rows = piece.shape[0]
    block_ids = jnp.arange(piece_rows, dtype=jnp.int32) // block_rows + 1
    allowed = segment[None, :] == block_ids[:, None]
    query_heads = piece.reshape(piece_rows, H, HEAD_DIM).transpose(1, 0, 2)

    def one_head(item):
        query_head, key_head, value_head = item
        score = (
            jnp.einsum("re,fe->rf", query_head, key_head, preferred_element_type=jnp.float32)
            * scale
        )
        score = jnp.where(allowed, score, NEG)
        block_max = jnp.max(score, axis=1)
        weights = jnp.where(allowed, jnp.exp(score - block_max[:, None]), 0.0)
        block_total = jnp.sum(weights, axis=1)
        summed = jnp.dot(
            weights.astype(jnp.bfloat16), value_head, preferred_element_type=jnp.float32
        )
        return (block_max, block_total, summed)

    block_max, block_total, summed = lax.map(one_head, (query_heads, key_heads, value_heads))
    run_max = block_max.T
    run_total = block_total.T
    joined = summed.transpose(1, 0, 2).reshape(piece_rows, feature_width)
    run_acc = joined
    run_max, run_total, run_acc = (run_max, run_total, run_acc)
    sources = lax.axis_size("frame")
    got_acc, got_max, got_total = (
        lax.all_to_all(
            run_acc.reshape(sources, owned_rows, feature_width),
            "frame",
            split_axis=0,
            concat_axis=0,
            tiled=True,
        ),
        lax.all_to_all(
            run_max.reshape(sources, owned_rows, H),
            "frame",
            split_axis=0,
            concat_axis=0,
            tiled=True,
        ),
        lax.all_to_all(
            run_total.reshape(sources, owned_rows, H),
            "frame",
            split_axis=0,
            concat_axis=0,
            tiled=True,
        ),
    )
    global_max = jnp.max(got_max, axis=0)
    factor = jnp.exp(got_max - global_max[None])
    norms = jnp.sum(got_total * factor, axis=0)
    sums = jnp.sum(
        got_acc.reshape(sources, owned_rows, H, HEAD_DIM) * factor[:, :, :, None], axis=0
    )
    cross = (sums / norms[:, :, None]).reshape(owned_rows, feature_width)
    cross = cross.astype(jnp.bfloat16)
    mixed = latent_full + jnp.dot(cross, w_cross_out, preferred_element_type=jnp.float32)
    normed_latent = layer_norm(mixed).astype(jnp.bfloat16)
    triple = jnp.dot(normed_latent, w_self_qkv, preferred_element_type=jnp.float32).astype(
        jnp.bfloat16
    )
    self_query = triple[:, :feature_width].reshape(owned_rows, H, HEAD_DIM)
    self_key = triple[:, feature_width : 2 * feature_width]
    self_value = triple[:, 2 * feature_width :]
    every_key, every_value = (
        lax.all_gather(self_key, "frame", axis=0, tiled=True),
        lax.all_gather(self_value, "frame", axis=0, tiled=True),
    )
    every_key = every_key.reshape(total_rows, H, HEAD_DIM)
    every_value = every_value.reshape(total_rows, H, HEAD_DIM)
    score = (
        jnp.einsum("rhe,mhe->hrm", self_query, every_key, preferred_element_type=jnp.float32)
        * scale
    )
    peak = jnp.max(score, axis=2, keepdims=True)
    expo = jnp.exp(score - peak)
    probs = (expo / jnp.sum(expo, axis=2, keepdims=True)).astype(jnp.bfloat16)
    attended = jnp.einsum("hrm,mhe->rhe", probs, every_value, preferred_element_type=jnp.float32)
    attended = attended.reshape(owned_rows, feature_width).astype(jnp.bfloat16)
    return (mixed + jnp.dot(attended, w_self_out, preferred_element_type=jnp.float32)).astype(
        jnp.bfloat16
    )


RUN = 64
PAD = 8
GROUP = 4
LATE = 2
WIDE = 256
PAIR = 2 * HEAD_DIM
BF16 = jnp.bfloat16
F32 = jnp.float32
VMEM = pltpu.VMEM


def norm(v):
    centre = v - jnp.mean(v, axis=-1, keepdims=True)
    spread = jnp.mean(centre * centre, axis=-1, keepdims=True)
    return centre * lax.rsqrt(spread + 1e-05)


def fill_stacks(stacks, j, blocks):
    for q in range(WIDE // PAIR):
        i = j * (WIDE // PAIR) + q
        wide = stacks.shape[2] // 2
        at = 0
        for block in blocks:
            turned = block[:, q * PAIR : (q + 1) * PAIR].T
            n = turned.shape[1]
            none = jnp.zeros((HEAD_DIM, n), BF16)
            stacks[i, :HEAD_DIM, at : at + n] = turned[:HEAD_DIM]
            stacks[i, HEAD_DIM:, at : at + n] = none
            stacks[i, :HEAD_DIM, wide + at : wide + at + n] = none
            stacks[i, HEAD_DIM:, wide + at : wide + at + n] = turned[HEAD_DIM:]
            at += n


def project(normed, weights, at, width, keys, values):
    n = normed.shape[0]
    for j in range(width // WIDE):
        cols = slice(j * WIDE, (j + 1) * WIDE)
        k = jnp.dot(normed, weights[:, at + j * WIDE : at + (j + 1) * WIDE], preferred_element_type=F32)
        keys[:n, cols] = k.astype(BF16)
        v = jnp.dot(
            normed, weights[:, at + width + j * WIDE : at + width + (j + 1) * WIDE], preferred_element_type=F32
        )
        values[cols, :n] = v.astype(BF16).T


def attend(n, left, stacks, keys, values, scores, probs, old, new):
    pairs, wide = stacks.shape[0], stacks.shape[2]
    half = wide // 2
    tops, totals, accs = new
    masked = left is not None
    if masked:
        valid = lax.broadcasted_iota(jnp.int32, (n, wide), 0) < left
    for i in range(pairs):
        score = jnp.dot(keys[:n, i * PAIR : (i + 1) * PAIR], stacks[i], preferred_element_type=F32)
        if masked:
            score = jnp.where(valid, score, NEG)
        scores[i, :n] = score
        top = jnp.max(score, axis=0, keepdims=True)
        tops[i : i + 1] = top if old is None else jnp.maximum(old[0][i : i + 1], top)
    for i in range(pairs):
        top = tops[i : i + 1]
        weights = jnp.exp(scores[i, :n] - top)
        if masked:
            weights = jnp.where(valid, weights, 0.0)
        total = jnp.sum(weights, axis=0, keepdims=True)
        if old is not None:
            total = total + old[1][i : i + 1] * jnp.exp(old[0][i : i + 1] - top)
        totals[i : i + 1] = total
        probs[i, :n] = weights.astype(BF16)
    for i in range(pairs):
        out = jnp.dot(values[i * PAIR : (i + 1) * PAIR, :n], probs[i, :n], preferred_element_type=F32)
        if old is not None:
            fade = jnp.exp(old[0][i : i + 1] - tops[i : i + 1])
        for h in range(2):
            rows = slice(i * PAIR + h * HEAD_DIM, i * PAIR + (h + 1) * HEAD_DIM)
            cols = slice(h * half, (h + 1) * half)
            part = out[h * HEAD_DIM : (h + 1) * HEAD_DIM, cols]
            if old is not None:
                part = part + old[2][rows, :] * fade[:, cols]
            accs[rows, :] = part


def tag_kernel(segment, frames, out, labels, sems):
    parts = [(frames.at[:RUN], out.at[:RUN]), (frames.at[RUN:], out.at[RUN + PAD :]), (segment, labels)]
    copies = [pltpu.make_async_copy(src, dst, sems.at[i]) for i, (src, dst) in enumerate(parts)]
    for copy in copies:
        copy.start()
    copies[2].wait()
    upper = lax.broadcasted_iota(jnp.int32, (PAD, out.shape[1]), 0) < PAD // 2
    out[RUN : RUN + PAD] = jnp.where(upper, labels[0].astype(F32), labels[RUN].astype(F32)).astype(BF16)
    copies[0].wait()
    copies[1].wait()


def queries_kernel(queries, stacks):
    scale = 1.0 / math.sqrt(HEAD_DIM)
    for j in range(queries.shape[1] // WIDE):
        block = queries[:, j * WIDE : (j + 1) * WIDE].astype(F32) * scale
        fill_stacks(stacks, j, [block.astype(BF16)])


def pick_runs(pieces, mine, picked, count):
    ids = [
        jnp.max(ref[label - label % PAD : label - label % PAD + PAD, :128][label % PAD : label % PAD + PAD // 2].astype(F32))
        for ref, spots in pieces for _, label in spots
    ]
    spots = [(ref, row) for ref, places in pieces for row, _ in places]
    count[0] = 0
    for label, (ref, row) in zip(ids, spots):
        @pl.when(label.astype(jnp.int32) == mine)
        def _(ref=ref, row=row):
            at = count[0]
            picked[at] = ref[row : row + RUN, :]
            count[0] = at + 1
    found = count[0]
    for extra in range(GROUP - 1):
        picked[found + extra] = jnp.zeros(picked.shape[1:], BF16)
    return found


def cross_groups(found, group, picked, w_kv, stacks, keys, values, scores, probs, state):
    width = state[2].shape[0]

    def one_group(g, carry):
        n = group * RUN
        frames = picked[pl.ds(g * group, group)].reshape(n, picked.shape[2])
        project(norm(frames.astype(F32)).astype(BF16), w_kv, 0, width, keys, values)
        old = (state[0][...], state[1][...], state[2])
        attend(n, (found - g * group) * RUN, stacks, keys, values, scores, probs, old, state)
        return carry

    lax.fori_loop(0, (found + group - 1) // group, one_group, 0)


def places(shape):
    if shape[0] == 2 * RUN + PAD:
        return [(0, RUN), (RUN + PAD, RUN + PAD // 2)]
    return None


def early_kernel(n_pieces, rows, *refs):
    pieces = [(ref, places(ref.shape)) for ref in refs[:n_pieces]]
    stacks, w_kv, tops, totals, accs, picked, keys, values, scores, probs, count = refs[n_pieces:]
    mine = (lax.axis_index("frame") * rows) // (L // NB) + 1
    tops[...] = jnp.full(tops.shape, NEG, F32)
    totals[...] = jnp.zeros(totals.shape, F32)
    accs[...] = jnp.zeros(accs.shape, F32)
    found = pick_runs(pieces, mine, picked, count)
    cross_groups(found, GROUP, picked, w_kv, stacks, keys, values, scores, probs, (tops, totals, accs))


def cross_kernel(n_pieces, *refs):
    (latents, stacks, w_kv, w_out, old_tops, old_totals, _, mixed_out, normed_out, tops, totals, accs,
     picked, keys, values, scores, probs, joined, count) = refs[n_pieces:]
    rows, _ = latents.shape
    mine = (lax.axis_index("frame") * rows) // (L // NB) + 1
    pieces = []
    for at, ref in enumerate(refs[:n_pieces]):
        half = [(0, RUN)] if at % 2 == 0 else [(PAD, PAD // 2)]
        pieces.append((ref, places(ref.shape) or half))
    tops[...], totals[...] = old_tops[...], old_totals[...]
    found = pick_runs(pieces, mine, picked, count)
    cross_groups(found, LATE, picked, w_kv, stacks, keys, values, scores, probs, (tops, totals, accs))
    finish(accs, totals, joined)
    mixed = latents[...].astype(F32) + jnp.dot(joined[...], w_out[...], preferred_element_type=F32)
    mixed_out[...] = mixed
    normed_out[...] = norm(mixed).astype(BF16)


def finish(accs, totals, joined):
    half = totals.shape[1] // 2
    for i in range(totals.shape[0]):
        parts = []
        for h in range(2):
            rows = slice(i * PAIR + h * HEAD_DIM, i * PAIR + (h + 1) * HEAD_DIM)
            parts.append(accs[rows, :] / totals[i : i + 1, h * half : (h + 1) * half])
        joined[:, i * PAIR : (i + 1) * PAIR] = jnp.concatenate(parts, axis=0).astype(BF16).T


def first_kernel(mine, other, w_qkv, stacks, tops, totals, accs, keys, values, scores, probs):
    rows, width = mine.shape
    scale = 1.0 / math.sqrt(HEAD_DIM)
    both = jnp.concatenate([mine[...], other[...]], axis=0)
    for j in range(width // WIDE):
        query = jnp.dot(both, w_qkv[:, j * WIDE : (j + 1) * WIDE], preferred_element_type=F32).astype(BF16)
        fill_stacks(stacks, j, [(query.astype(F32) * scale).astype(BF16)])
    project(mine[...], w_qkv, width, width, keys, values)
    attend(rows, None, stacks, keys, values, scores, probs, None, (tops, totals, accs))


def next_kernel(n_pieces, *refs):
    sources = refs[:n_pieces]
    (w_qkv, stacks, old_tops, old_totals, old_accs, tops, totals, accs, keys, values, scores, probs) = refs[n_pieces:]
    width = accs.shape[0]
    block = jnp.concatenate([s[...] for s in sources], axis=0)
    project(block, w_qkv, width, width, keys, values)
    old = (old_tops[...], old_totals[...], old_accs)
    attend(block.shape[0], None, stacks, keys, values, scores, probs, old, (tops, totals, accs))


def final_kernel(tops, totals, accs, far, mixed, w_out, out, joined, merged, sums):
    width, rows = far.shape[0] - 2 * 2 * tops.shape[0], far.shape[1]
    for i in range(tops.shape[0]):
        for h in range(2):
            at = 2 * i + h
            here = slice(h * 2 * rows, h * 2 * rows + rows)
            lines = slice(i * PAIR + h * HEAD_DIM, i * PAIR + (h + 1) * HEAD_DIM)
            near_top, far_top = tops[i : i + 1, here], far[width + at : width + at + 1]
            top = jnp.maximum(near_top, far_top)
            near_fade, far_fade = jnp.exp(near_top - top), jnp.exp(far_top - top)
            far_total = far[width + 2 * tops.shape[0] + at : width + 2 * tops.shape[0] + at + 1]
            sums[i : i + 1, h * rows : (h + 1) * rows] = totals[i : i + 1, here] * near_fade + far_total * far_fade
            merged[lines] = accs[lines, :rows] * near_fade + far[lines] * far_fade
    finish(merged, sums, joined)
    out[...] = (mixed[...] + jnp.dot(joined[...], w_out[...], preferred_element_type=F32)).astype(BF16)


def last_kernel(n_pieces, *refs):
    sources = refs[:n_pieces]
    (w_qkv, stacks, old_tops, old_totals, old_accs, tops, totals, accs, away,
     keys, values, scores, probs) = refs[n_pieces:]
    next_kernel(n_pieces, *sources, w_qkv, stacks, old_tops, old_totals, old_accs, tops, totals, accs,
                keys, values, scores, probs)
    width, rows = accs.shape[0], accs.shape[1] // 2
    away[:width] = accs[:, rows:]
    for i in range(tops.shape[0]):
        for h in range(2):
            there = slice(h * 2 * rows + rows, (h + 1) * 2 * rows)
            at = 2 * i + h
            away[width + at : width + at + 1] = tops[i : i + 1, there]
            at += 2 * tops.shape[0]
            away[width + at : width + at + 1] = totals[i : i + 1, there]


def on_chip(x):
    return pltpu.with_memory_space_constraint(x, VMEM)


def call(kernel, args, outs, scratch, flops, limit, aliases=None, scalars=0):
    specs = [pl.BlockSpec(memory_space=pltpu.SMEM)] * scalars
    specs += [pl.BlockSpec(memory_space=VMEM)] * (len(args) - scalars)
    return pl.pallas_call(
        kernel,
        out_shape=outs,
        in_specs=specs,
        out_specs=jax.tree.map(lambda _: pl.BlockSpec(memory_space=VMEM), outs, is_leaf=lambda o: hasattr(o, "shape")),
        scratch_shapes=scratch,
        compiler_params=pltpu.CompilerParams(vmem_limit_bytes=limit << 20),
        cost_estimate=pl.CostEstimate(flops=flops, bytes_accessed=1 << 20, transcendentals=0),
        input_output_aliases=aliases or {},
    )(*args[:scalars], *[on_chip(a) for a in args[scalars:]])


def shards_ring(frames, segment, latents, latent_queries, w_kv, w_cross_out, w_self_qkv, w_self_out):
    chips = lax.axis_size("frame") // 2
    rows, width = latents.shape
    channels = frames.shape[1]
    order = [2 * k for k in range(chips // 2)] + [2 * k + 1 for k in reversed(range(chips // 2))]
    swap = [(i, i ^ 1) for i in range(2 * chips)]
    ahead = [(2 * order[k] + c, 2 * order[(k + 1) % chips] + c) for k in range(chips) for c in range(2)]
    behind = [(there, here) for here, there in ahead]

    def cross_over(x):
        return lax.ppermute(x, "frame", swap)

    def both_ways(fore, aft):
        fore = lax.ppermute(fore, "frame", ahead)
        aft = lax.ppermute(aft, "frame", behind)
        return fore, aft

    def swapped(fore, aft):
        fore = cross_over(fore)
        aft = cross_over(aft)
        return fore, aft

    def ring(x):
        fore, aft = x, x
        found = []
        for _ in range(1, chips // 2):
            fore, aft = both_ways(fore, aft)
            found.append([fore, aft])
        cut = x.shape[0] // 2
        return found + [list(both_ways(fore[:cut], aft[cut:]))]

    def gather(tagged):
        cut = tagged.shape[0] // 2 + PAD // 2
        found = [[tagged, cross_over(tagged)]]
        fore, aft = tagged, tagged
        for _ in range(1, chips // 2):
            fore, aft = both_ways(fore, aft)
            found.append([fore, aft, *swapped(fore, aft)])
        fore, aft = both_ways(fore[:cut], aft[-cut:])
        return found + [[fore, aft, cross_over(fore), cross_over(aft)]]

    pairs = width // PAIR
    tagged = pl.pallas_call(
        tag_kernel,
        out_shape=VMEM((frames.shape[0] + PAD, channels), BF16),
        in_specs=[pl.BlockSpec(memory_space=pl.ANY)] * 2,
        out_specs=pl.BlockSpec(memory_space=VMEM),
        scratch_shapes=[pltpu.SMEM(segment.shape, jnp.int32), pltpu.SemaphoreType.DMA((3,))],
        compiler_params=pltpu.CompilerParams(vmem_limit_bytes=2 << 20),
        cost_estimate=pl.CostEstimate(flops=1 << 34, bytes_accessed=1 << 20, transcendentals=0),
        name="tag",
    )(*[pltpu.with_memory_space_constraint(x, pltpu.HBM) for x in (segment, frames)])
    stacks = call(queries_kernel, [latent_queries], VMEM((pairs, PAIR, 2 * rows), BF16), [], 1 << 28, 4)

    def state(queries):
        return (VMEM((pairs, 2 * queries), F32), VMEM((pairs, 2 * queries), F32), VMEM((width, queries), F32))

    def work(n, queries):
        return [
            VMEM((n, width), BF16), VMEM((width, n), BF16),
            VMEM((pairs, n, 2 * queries), F32), VMEM((pairs, n, 2 * queries), BF16),
        ]

    pieces = gather(tagged)
    soon = [piece for group in pieces[:-2] for piece in group]
    late = [piece for group in pieces[-2:] for piece in group]
    kept = call(
        functools.partial(early_kernel, len(soon), rows), soon + [stacks, w_kv], state(rows),
        [VMEM((2 * len(soon) + GROUP, RUN, channels), BF16), *work(GROUP * RUN, rows), pltpu.SMEM((1,), jnp.int32)],
        1 << 30, 16,
    )
    n = len(late)
    mixed, normed, *_ = call(
        functools.partial(cross_kernel, n),
        late + [latents, stacks, w_kv, w_cross_out, *kept],
        (VMEM((rows, width), F32), VMEM((rows, width), BF16), *state(rows)),
        [
            VMEM((2 * n + GROUP, RUN, channels), BF16), *work(LATE * RUN, rows),
            VMEM((rows, width), BF16), pltpu.SMEM((1,), jnp.int32),
        ],
        4 << 30, 16, {n + 4: 2, n + 5: 3, n + 6: 4},
    )
    arrivals = ring(normed)
    stacks, *kept = call(
        first_kernel, [normed, cross_over(normed), w_self_qkv],
        (VMEM((pairs, PAIR, 4 * rows), BF16), *state(2 * rows)), work(rows, 2 * rows), 1 << 30, 16,
    )
    for sources in arrivals[:-1]:
        n = len(sources)
        kept = call(
            functools.partial(next_kernel, n), sources + [w_self_qkv, stacks, *kept],
            state(2 * rows), work(n * rows, 2 * rows), n << 30, 20, {n + 2: 0, n + 3: 1, n + 4: 2},
        )
    sources = arrivals[-1]
    n = len(sources)
    *kept, away = call(
        functools.partial(last_kernel, n), sources + [w_self_qkv, stacks, *kept],
        (*state(2 * rows), VMEM((width + 4 * pairs, rows), F32)), work(rows, 2 * rows), 1 << 30, 20,
        {n + 2: 0, n + 3: 1, n + 4: 2},
    )
    return call(
        final_kernel, [*kept, cross_over(away), mixed, w_self_out],
        jax.ShapeDtypeStruct((rows, width), BF16),
        [VMEM((rows, width), BF16), VMEM((width, rows), F32), VMEM((pairs, 2 * rows), F32)],
        1 << 30, 12,
    )


def solution(mesh):
    placed = (
        P(("rep", "frame"), None),
        P(("rep", "frame")),
        P("frame", None),
        P("frame", None),
        P(),
        P(),
        P(),
        P(),
    )
    if mesh.shape["frame"] != 16:
        return jax.shard_map(
            shards_any, mesh=mesh, in_specs=placed, out_specs=P(("rep", "frame"), None), check_vma=False
        )

    return jax.shard_map(shards_ring, mesh=mesh, in_specs=placed, out_specs=P(("rep", "frame"), None), check_vma=False)
```

```python
import functools
import math

import jax
import jax.numpy as jnp
from jax import lax
from jax.experimental import pallas as pl
from jax.experimental.pallas import tpu as pltpu
from jax.sharding import PartitionSpec as P

H = 16
HEAD_DIM = 64
L = 2048
NB = 8


NEG = -1e30


def layer_norm(inputs):
    centre = inputs - jnp.mean(inputs, axis=-1, keepdims=True)
    spread = jnp.mean(centre * centre, axis=-1, keepdims=True)
    return centre * lax.rsqrt(spread + 1e-05)


def shards_any(frames, segment, latents, latent_queries, w_kv, w_cross_out, w_self_qkv, w_self_out):
    feature_width = w_kv.shape[1] // 2
    owned_rows = latents.shape[0]
    frame_count = frames.shape[0]
    scale = 1.0 / math.sqrt(HEAD_DIM)
    block_rows = L // NB
    latent_full = latents.astype(jnp.float32)
    normed = layer_norm(frames.astype(jnp.float32)).astype(jnp.bfloat16)
    keyval = jnp.dot(normed, w_kv, preferred_element_type=jnp.float32).astype(jnp.bfloat16)
    key_heads = keyval[:, :feature_width].reshape(frame_count, H, HEAD_DIM).transpose(1, 0, 2)
    value_heads = keyval[:, feature_width:].reshape(frame_count, H, HEAD_DIM).transpose(1, 0, 2)
    total_rows = owned_rows * lax.axis_size("frame")
    piece = lax.all_gather(latent_queries, "frame", axis=0, tiled=True)
    piece_rows = piece.shape[0]
    block_ids = jnp.arange(piece_rows, dtype=jnp.int32) // block_rows + 1
    allowed = segment[None, :] == block_ids[:, None]
    query_heads = piece.reshape(piece_rows, H, HEAD_DIM).transpose(1, 0, 2)

    def one_head(item):
        query_head, key_head, value_head = item
        score = (
            jnp.einsum("re,fe->rf", query_head, key_head, preferred_element_type=jnp.float32)
            * scale
        )
        score = jnp.where(allowed, score, NEG)
        block_max = jnp.max(score, axis=1)
        weights = jnp.where(allowed, jnp.exp(score - block_max[:, None]), 0.0)
        block_total = jnp.sum(weights, axis=1)
        summed = jnp.dot(
            weights.astype(jnp.bfloat16), value_head, preferred_element_type=jnp.float32
        )
        return (block_max, block_total, summed)

    block_max, block_total, summed = lax.map(one_head, (query_heads, key_heads, value_heads))
    run_max = block_max.T
    run_total = block_total.T
    joined = summed.transpose(1, 0, 2).reshape(piece_rows, feature_width)
    run_acc = joined
    run_max, run_total, run_acc = (run_max, run_total, run_acc)
    sources = lax.axis_size("frame")
    got_acc, got_max, got_total = (
        lax.all_to_all(
            run_acc.reshape(sources, owned_rows, feature_width),
            "frame",
            split_axis=0,
            concat_axis=0,
            tiled=True,
        ),
        lax.all_to_all(
            run_max.reshape(sources, owned_rows, H),
            "frame",
            split_axis=0,
            concat_axis=0,
            tiled=True,
        ),
        lax.all_to_all(
            run_total.reshape(sources, owned_rows, H),
            "frame",
            split_axis=0,
            concat_axis=0,
            tiled=True,
        ),
    )
    global_max = jnp.max(got_max, axis=0)
    factor = jnp.exp(got_max - global_max[None])
    norms = jnp.sum(got_total * factor, axis=0)
    sums = jnp.sum(
        got_acc.reshape(sources, owned_rows, H, HEAD_DIM) * factor[:, :, :, None], axis=0
    )
    cross = (sums / norms[:, :, None]).reshape(owned_rows, feature_width)
    cross = cross.astype(jnp.bfloat16)
    mixed = latent_full + jnp.dot(cross, w_cross_out, preferred_element_type=jnp.float32)
    normed_latent = layer_norm(mixed).astype(jnp.bfloat16)
    triple = jnp.dot(normed_latent, w_self_qkv, preferred_element_type=jnp.float32).astype(
        jnp.bfloat16
    )
    self_query = triple[:, :feature_width].reshape(owned_rows, H, HEAD_DIM)
    self_key = triple[:, feature_width : 2 * feature_width]
    self_value = triple[:, 2 * feature_width :]
    every_key, every_value = (
        lax.all_gather(self_key, "frame", axis=0, tiled=True),
        lax.all_gather(self_value, "frame", axis=0, tiled=True),
    )
    every_key = every_key.reshape(total_rows, H, HEAD_DIM)
    every_value = every_value.reshape(total_rows, H, HEAD_DIM)
    score = (
        jnp.einsum("rhe,mhe->hrm", self_query, every_key, preferred_element_type=jnp.float32)
        * scale
    )
    peak = jnp.max(score, axis=2, keepdims=True)
    expo = jnp.exp(score - peak)
    probs = (expo / jnp.sum(expo, axis=2, keepdims=True)).astype(jnp.bfloat16)
    attended = jnp.einsum("hrm,mhe->rhe", probs, every_value, preferred_element_type=jnp.float32)
    attended = attended.reshape(owned_rows, feature_width).astype(jnp.bfloat16)
    return (mixed + jnp.dot(attended, w_self_out, preferred_element_type=jnp.float32)).astype(
        jnp.bfloat16
    )


RUN = 64
PAD = 8
GROUP = 2
WIDE = 256
PAIR = 2 * HEAD_DIM
BF16 = jnp.bfloat16
F32 = jnp.float32
VMEM = pltpu.VMEM


def norm(v):
    centre = v - jnp.mean(v, axis=-1, keepdims=True)
    spread = jnp.mean(centre * centre, axis=-1, keepdims=True)
    return centre * lax.rsqrt(spread + 1e-05)


def fill_stacks(stacks, j, blocks):
    for q in range(WIDE // PAIR):
        i = j * (WIDE // PAIR) + q
        wide = stacks.shape[2] // 2
        at = 0
        for block in blocks:
            turned = block[:, q * PAIR : (q + 1) * PAIR].T
            n = turned.shape[1]
            none = jnp.zeros((HEAD_DIM, n), BF16)
            stacks[i, :HEAD_DIM, at : at + n] = turned[:HEAD_DIM]
            stacks[i, HEAD_DIM:, at : at + n] = none
            stacks[i, :HEAD_DIM, wide + at : wide + at + n] = none
            stacks[i, HEAD_DIM:, wide + at : wide + at + n] = turned[HEAD_DIM:]
            at += n


def project(normed, weights, at, width, keys, values):
    n = normed.shape[0]
    for j in range(width // WIDE):
        cols = slice(j * WIDE, (j + 1) * WIDE)
        k = jnp.dot(normed, weights[:, at + j * WIDE : at + (j + 1) * WIDE], preferred_element_type=F32)
        keys[:n, cols] = k.astype(BF16)
        v = jnp.dot(
            normed, weights[:, at + width + j * WIDE : at + width + (j + 1) * WIDE], preferred_element_type=F32
        )
        values[cols, :n] = v.astype(BF16).T


def attend(n, left, stacks, keys, values, scores, probs, old, new):
    pairs, wide = stacks.shape[0], stacks.shape[2]
    half = wide // 2
    tops, totals, accs = new
    masked = left is not None
    if masked:
        valid = lax.broadcasted_iota(jnp.int32, (n, wide), 0) < left
    for i in range(pairs):
        score = jnp.dot(keys[:n, i * PAIR : (i + 1) * PAIR], stacks[i], preferred_element_type=F32)
        if masked:
            score = jnp.where(valid, score, NEG)
        scores[i, :n] = score
        top = jnp.max(score, axis=0, keepdims=True)
        tops[i : i + 1] = top if old is None else jnp.maximum(old[0][i : i + 1], top)
    for i in range(pairs):
        top = tops[i : i + 1]
        weights = jnp.exp(scores[i, :n] - top)
        if masked:
            weights = jnp.where(valid, weights, 0.0)
        total = jnp.sum(weights, axis=0, keepdims=True)
        if old is not None:
            total = total + old[1][i : i + 1] * jnp.exp(old[0][i : i + 1] - top)
        totals[i : i + 1] = total
        probs[i, :n] = weights.astype(BF16)
    for i in range(pairs):
        out = jnp.dot(values[i * PAIR : (i + 1) * PAIR, :n], probs[i, :n], preferred_element_type=F32)
        if old is not None:
            fade = jnp.exp(old[0][i : i + 1] - tops[i : i + 1])
        for h in range(2):
            rows = slice(i * PAIR + h * HEAD_DIM, i * PAIR + (h + 1) * HEAD_DIM)
            cols = slice(h * half, (h + 1) * half)
            part = out[h * HEAD_DIM : (h + 1) * HEAD_DIM, cols]
            if old is not None:
                part = part + old[2][rows, :] * fade[:, cols]
            accs[rows, :] = part


def tag_kernel(segment, frames, out, labels, sems):
    parts = [(frames.at[:RUN], out.at[:RUN]), (frames.at[RUN:], out.at[RUN + PAD :]), (segment, labels)]
    copies = [pltpu.make_async_copy(src, dst, sems.at[i]) for i, (src, dst) in enumerate(parts)]
    for copy in copies:
        copy.start()
    copies[2].wait()
    upper = lax.broadcasted_iota(jnp.int32, (PAD, out.shape[1]), 0) < PAD // 2
    out[RUN : RUN + PAD] = jnp.where(upper, labels[0].astype(F32), labels[RUN].astype(F32)).astype(BF16)
    copies[0].wait()
    copies[1].wait()


def queries_kernel(queries, stacks):
    scale = 1.0 / math.sqrt(HEAD_DIM)
    for j in range(queries.shape[1] // WIDE):
        block = queries[:, j * WIDE : (j + 1) * WIDE].astype(F32) * scale
        fill_stacks(stacks, j, [block.astype(BF16)])


def pick_runs(pieces, mine, picked, count):
    ids = [
        jnp.max(ref[label - label % PAD : label - label % PAD + PAD, :128][label % PAD : label % PAD + PAD // 2].astype(F32))
        for ref, spots in pieces for _, label in spots
    ]
    spots = [(ref, row) for ref, places in pieces for row, _ in places]
    count[0] = 0
    for label, (ref, row) in zip(ids, spots):
        @pl.when(label.astype(jnp.int32) == mine)
        def _(ref=ref, row=row):
            at = count[0]
            picked[at] = ref[row : row + RUN, :]
            count[0] = at + 1
    found = count[0]
    for extra in range(GROUP - 1):
        picked[found + extra] = jnp.zeros(picked.shape[1:], BF16)
    return found


def cross_groups(found, group, picked, w_kv, stacks, keys, values, scores, probs, state):
    width = state[2].shape[0]

    def one_group(g, carry):
        n = group * RUN
        frames = picked[pl.ds(g * group, group)].reshape(n, picked.shape[2])
        project(norm(frames.astype(F32)).astype(BF16), w_kv, 0, width, keys, values)
        old = (state[0][...], state[1][...], state[2])
        attend(n, (found - g * group) * RUN, stacks, keys, values, scores, probs, old, state)
        return carry

    lax.fori_loop(0, (found + group - 1) // group, one_group, 0)


def places(shape):
    if shape[0] == 2 * RUN + PAD:
        return [(0, RUN), (RUN + PAD, RUN + PAD // 2)]
    return None


def early_kernel(n_pieces, rows, *refs):
    pieces = [(ref, places(ref.shape)) for ref in refs[:n_pieces]]
    stacks, w_kv, *old = refs[n_pieces : len(refs) - 9]
    tops, totals, accs, picked, keys, values, scores, probs, count = refs[len(refs) - 9 :]
    mine = (lax.axis_index("frame") * rows) // (L // NB) + 1
    if old:
        tops[...], totals[...] = old[0][...], old[1][...]
    else:
        tops[...] = jnp.full(tops.shape, NEG, F32)
        totals[...] = jnp.zeros(totals.shape, F32)
        accs[...] = jnp.zeros(accs.shape, F32)
    found = pick_runs(pieces, mine, picked, count)
    cross_groups(found, GROUP, picked, w_kv, stacks, keys, values, scores, probs, (tops, totals, accs))


def cross_kernel(n_pieces, *refs):
    (latents, stacks, w_kv, w_out, old_tops, old_totals, _, mixed_out, normed_out, tops, totals, accs,
     picked, keys, values, scores, probs, joined, count) = refs[n_pieces:]
    rows, _ = latents.shape
    mine = (lax.axis_index("frame") * rows) // (L // NB) + 1
    pieces = []
    for at, ref in enumerate(refs[:n_pieces]):
        half = [(0, RUN)] if at % 2 == 0 else [(PAD, PAD // 2)]
        pieces.append((ref, places(ref.shape) or half))
    tops[...], totals[...] = old_tops[...], old_totals[...]
    found = pick_runs(pieces, mine, picked, count)
    cross_groups(found, GROUP, picked, w_kv, stacks, keys, values, scores, probs, (tops, totals, accs))
    finish(accs, totals, joined)
    mixed = latents[...].astype(F32) + jnp.dot(joined[...], w_out[...], preferred_element_type=F32)
    mixed_out[...] = mixed
    normed_out[...] = norm(mixed).astype(BF16)


def finish(accs, totals, joined):
    half = totals.shape[1] // 2
    for i in range(totals.shape[0]):
        parts = []
        for h in range(2):
            rows = slice(i * PAIR + h * HEAD_DIM, i * PAIR + (h + 1) * HEAD_DIM)
            parts.append(accs[rows, :] / totals[i : i + 1, h * half : (h + 1) * half])
        joined[:, i * PAIR : (i + 1) * PAIR] = jnp.concatenate(parts, axis=0).astype(BF16).T


def first_kernel(mine, other, w_qkv, stacks, tops, totals, accs, keys, values, scores, probs):
    rows, width = mine.shape
    scale = 1.0 / math.sqrt(HEAD_DIM)
    both = jnp.concatenate([mine[...], other[...]], axis=0)
    for j in range(width // WIDE):
        query = jnp.dot(both, w_qkv[:, j * WIDE : (j + 1) * WIDE], preferred_element_type=F32).astype(BF16)
        fill_stacks(stacks, j, [(query.astype(F32) * scale).astype(BF16)])
    project(mine[...], w_qkv, width, width, keys, values)
    attend(rows, None, stacks, keys, values, scores, probs, None, (tops, totals, accs))


def next_kernel(n_pieces, *refs):
    sources = refs[:n_pieces]
    (w_qkv, stacks, old_tops, old_totals, old_accs, tops, totals, accs, keys, values, scores, probs) = refs[n_pieces:]
    width = accs.shape[0]
    block = jnp.concatenate([s[...] for s in sources], axis=0)
    project(block, w_qkv, width, width, keys, values)
    old = (old_tops[...], old_totals[...], old_accs)
    attend(block.shape[0], None, stacks, keys, values, scores, probs, old, (tops, totals, accs))


def final_kernel(tops, totals, accs, far, mixed, w_out, out, joined, merged, sums):
    width, rows = far.shape[0] - 2 * 2 * tops.shape[0], far.shape[1]
    for i in range(tops.shape[0]):
        for h in range(2):
            at = 2 * i + h
            here = slice(h * 2 * rows, h * 2 * rows + rows)
            lines = slice(i * PAIR + h * HEAD_DIM, i * PAIR + (h + 1) * HEAD_DIM)
            near_top, far_top = tops[i : i + 1, here], far[width + at : width + at + 1]
            top = jnp.maximum(near_top, far_top)
            near_fade, far_fade = jnp.exp(near_top - top), jnp.exp(far_top - top)
            far_total = far[width + 2 * tops.shape[0] + at : width + 2 * tops.shape[0] + at + 1]
            sums[i : i + 1, h * rows : (h + 1) * rows] = totals[i : i + 1, here] * near_fade + far_total * far_fade
            merged[lines] = accs[lines, :rows] * near_fade + far[lines] * far_fade
    finish(merged, sums, joined)
    out[...] = (mixed[...] + jnp.dot(joined[...], w_out[...], preferred_element_type=F32)).astype(BF16)


def last_kernel(n_pieces, *refs):
    sources = refs[:n_pieces]
    (w_qkv, stacks, old_tops, old_totals, old_accs, tops, totals, accs, away,
     keys, values, scores, probs) = refs[n_pieces:]
    next_kernel(n_pieces, *sources, w_qkv, stacks, old_tops, old_totals, old_accs, tops, totals, accs,
                keys, values, scores, probs)
    width, rows = accs.shape[0], accs.shape[1] // 2
    away[:width] = accs[:, rows:]
    for i in range(tops.shape[0]):
        for h in range(2):
            there = slice(h * 2 * rows + rows, (h + 1) * 2 * rows)
            at = 2 * i + h
            away[width + at : width + at + 1] = tops[i : i + 1, there]
            at += 2 * tops.shape[0]
            away[width + at : width + at + 1] = totals[i : i + 1, there]


def on_chip(x):
    return pltpu.with_memory_space_constraint(x, VMEM)


def call(kernel, args, outs, scratch, flops, limit, aliases=None, scalars=0):
    specs = [pl.BlockSpec(memory_space=pltpu.SMEM)] * scalars
    specs += [pl.BlockSpec(memory_space=VMEM)] * (len(args) - scalars)
    return pl.pallas_call(
        kernel,
        out_shape=outs,
        in_specs=specs,
        out_specs=jax.tree.map(lambda _: pl.BlockSpec(memory_space=VMEM), outs, is_leaf=lambda o: hasattr(o, "shape")),
        scratch_shapes=scratch,
        compiler_params=pltpu.CompilerParams(vmem_limit_bytes=limit << 20),
        cost_estimate=pl.CostEstimate(flops=flops, bytes_accessed=1 << 20, transcendentals=0),
        input_output_aliases=aliases or {},
    )(*args[:scalars], *[on_chip(a) for a in args[scalars:]])


def shards_ring(frames, segment, latents, latent_queries, w_kv, w_cross_out, w_self_qkv, w_self_out):
    chips = lax.axis_size("frame") // 2
    rows, width = latents.shape
    channels = frames.shape[1]
    order = [2 * k for k in range(chips // 2)] + [2 * k + 1 for k in reversed(range(chips // 2))]
    swap = [(i, i ^ 1) for i in range(2 * chips)]
    ahead = [(2 * order[k] + c, 2 * order[(k + 1) % chips] + c) for k in range(chips) for c in range(2)]
    behind = [(there, here) for here, there in ahead]

    def cross_over(x):
        return lax.ppermute(x, "frame", swap)

    def both_ways(fore, aft):
        fore = lax.ppermute(fore, "frame", ahead)
        aft = lax.ppermute(aft, "frame", behind)
        return fore, aft

    def swapped(fore, aft):
        fore = cross_over(fore)
        aft = cross_over(aft)
        return fore, aft

    def ring(x):
        cut = x.shape[0] // 2
        red, blue = (x[:cut], x[cut:]), (x[cut:], x[:cut])
        reds, blues = [], []
        for _ in range(1, chips // 2):
            red = both_ways(*red)
            blue = both_ways(*blue)
            reds.append(list(red))
            blues.append(list(blue))
        reds.append(list(both_ways(*red)))
        return reds, blues

    def gather(tagged):
        cut = tagged.shape[0] // 2 + PAD // 2
        found = [[tagged, cross_over(tagged)]]
        fore, aft = tagged, tagged
        for _ in range(1, chips // 2):
            fore, aft = both_ways(fore, aft)
            found.append([fore, aft, *swapped(fore, aft)])
        fore, aft = both_ways(fore[:cut], aft[-cut:])
        return found + [[fore, aft, cross_over(fore), cross_over(aft)]]

    pairs = width // PAIR
    tagged = pl.pallas_call(
        tag_kernel,
        out_shape=VMEM((frames.shape[0] + PAD, channels), BF16),
        in_specs=[pl.BlockSpec(memory_space=pl.ANY)] * 2,
        out_specs=pl.BlockSpec(memory_space=VMEM),
        scratch_shapes=[pltpu.SMEM(segment.shape, jnp.int32), pltpu.SemaphoreType.DMA((3,))],
        compiler_params=pltpu.CompilerParams(vmem_limit_bytes=2 << 20),
        cost_estimate=pl.CostEstimate(flops=1 << 34, bytes_accessed=1 << 20, transcendentals=0),
        name="tag",
    )(*[pltpu.with_memory_space_constraint(x, pltpu.HBM) for x in (segment, frames)])
    stacks = call(queries_kernel, [latent_queries], VMEM((pairs, PAIR, 2 * rows), BF16), [], 1 << 28, 4)

    def state(queries):
        return (VMEM((pairs, 2 * queries), F32), VMEM((pairs, 2 * queries), F32), VMEM((width, queries), F32))

    def work(n, queries):
        return [
            VMEM((n, width), BF16), VMEM((width, n), BF16),
            VMEM((pairs, n, 2 * queries), F32), VMEM((pairs, n, 2 * queries), BF16),
        ]

    pieces = gather(tagged)
    late = pieces[-2] + pieces[-1]
    kept = []
    for soon in [pieces[0] + pieces[1], *pieces[2:-2]]:
        n = len(soon)
        kept = call(
            functools.partial(early_kernel, n, rows), soon + [stacks, w_kv, *kept], state(rows),
            [VMEM((2 * n + GROUP, RUN, channels), BF16), *work(GROUP * RUN, rows), pltpu.SMEM((1,), jnp.int32)],
            1 << 30, 16, {n + 2: 0, n + 3: 1, n + 4: 2} if kept else None,
        )
    n = len(late)
    mixed, normed, *_ = call(
        functools.partial(cross_kernel, n),
        late + [latents, stacks, w_kv, w_cross_out, *kept],
        (VMEM((rows, width), F32), VMEM((rows, width), BF16), *state(rows)),
        [
            VMEM((2 * n + GROUP, RUN, channels), BF16), *work(GROUP * RUN, rows),
            VMEM((rows, width), BF16), pltpu.SMEM((1,), jnp.int32),
        ],
        4 << 30, 16, {n + 4: 2, n + 5: 3, n + 6: 4},
    )
    reds, blues = ring(normed)
    arrivals = [reds[0]] + [blue + red for blue, red in zip(blues, reds[1:-1])] + [blues[-1], reds[-1]]
    stacks, *kept = call(
        first_kernel, [normed, cross_over(normed), w_self_qkv],
        (VMEM((pairs, PAIR, 4 * rows), BF16), *state(2 * rows)), work(rows, 2 * rows), 1 << 30, 16,
    )
    for sources in arrivals[:-1]:
        n = len(sources)
        keys = sum(source.shape[0] for source in sources)
        kept = call(
            functools.partial(next_kernel, n), sources + [w_self_qkv, stacks, *kept],
            state(2 * rows), work(keys, 2 * rows), n << 29, 20, {n + 2: 0, n + 3: 1, n + 4: 2},
        )
    sources = arrivals[-1]
    n = len(sources)
    *kept, away = call(
        functools.partial(last_kernel, n), sources + [w_self_qkv, stacks, *kept],
        (*state(2 * rows), VMEM((width + 4 * pairs, rows), F32)), work(rows, 2 * rows), 1 << 30, 20,
        {n + 2: 0, n + 3: 1, n + 4: 2},
    )
    return call(
        final_kernel, [*kept, cross_over(away), mixed, w_self_out],
        jax.ShapeDtypeStruct((rows, width), BF16),
        [VMEM((rows, width), BF16), VMEM((width, rows), F32), VMEM((pairs, 2 * rows), F32)],
        1 << 30, 12,
    )


def solution(mesh):
    placed = (
        P(("rep", "frame"), None),
        P(("rep", "frame")),
        P("frame", None),
        P("frame", None),
        P(),
        P(),
        P(),
        P(),
    )
    if mesh.shape["frame"] != 16:
        return jax.shard_map(
            shards_any, mesh=mesh, in_specs=placed, out_specs=P(("rep", "frame"), None), check_vma=False
        )

    return jax.shard_map(shards_ring, mesh=mesh, in_specs=placed, out_specs=P(("rep", "frame"), None), check_vma=False)
```

```python
import functools
import math

import jax
import jax.numpy as jnp
from jax import lax
from jax.experimental import pallas as pl
from jax.experimental.pallas import tpu as pltpu
from jax.sharding import PartitionSpec as P

H = 16
HEAD_DIM = 64
L = 2048
NB = 8


NEG = -1e30


def layer_norm(inputs):
    centre = inputs - jnp.mean(inputs, axis=-1, keepdims=True)
    spread = jnp.mean(centre * centre, axis=-1, keepdims=True)
    return centre * lax.rsqrt(spread + 1e-05)


def shards_any(frames, segment, latents, latent_queries, w_kv, w_cross_out, w_self_qkv, w_self_out):
    feature_width = w_kv.shape[1] // 2
    owned_rows = latents.shape[0]
    frame_count = frames.shape[0]
    scale = 1.0 / math.sqrt(HEAD_DIM)
    block_rows = L // NB
    latent_full = latents.astype(jnp.float32)
    normed = layer_norm(frames.astype(jnp.float32)).astype(jnp.bfloat16)
    keyval = jnp.dot(normed, w_kv, preferred_element_type=jnp.float32).astype(jnp.bfloat16)
    key_heads = keyval[:, :feature_width].reshape(frame_count, H, HEAD_DIM).transpose(1, 0, 2)
    value_heads = keyval[:, feature_width:].reshape(frame_count, H, HEAD_DIM).transpose(1, 0, 2)
    total_rows = owned_rows * lax.axis_size("frame")
    piece = lax.all_gather(latent_queries, "frame", axis=0, tiled=True)
    piece_rows = piece.shape[0]
    block_ids = jnp.arange(piece_rows, dtype=jnp.int32) // block_rows + 1
    allowed = segment[None, :] == block_ids[:, None]
    query_heads = piece.reshape(piece_rows, H, HEAD_DIM).transpose(1, 0, 2)

    def one_head(item):
        query_head, key_head, value_head = item
        score = (
            jnp.einsum("re,fe->rf", query_head, key_head, preferred_element_type=jnp.float32)
            * scale
        )
        score = jnp.where(allowed, score, NEG)
        block_max = jnp.max(score, axis=1)
        weights = jnp.where(allowed, jnp.exp(score - block_max[:, None]), 0.0)
        block_total = jnp.sum(weights, axis=1)
        summed = jnp.dot(
            weights.astype(jnp.bfloat16), value_head, preferred_element_type=jnp.float32
        )
        return (block_max, block_total, summed)

    block_max, block_total, summed = lax.map(one_head, (query_heads, key_heads, value_heads))
    run_max = block_max.T
    run_total = block_total.T
    joined = summed.transpose(1, 0, 2).reshape(piece_rows, feature_width)
    run_acc = joined
    run_max, run_total, run_acc = (run_max, run_total, run_acc)
    sources = lax.axis_size("frame")
    got_acc, got_max, got_total = (
        lax.all_to_all(
            run_acc.reshape(sources, owned_rows, feature_width),
            "frame",
            split_axis=0,
            concat_axis=0,
            tiled=True,
        ),
        lax.all_to_all(
            run_max.reshape(sources, owned_rows, H),
            "frame",
            split_axis=0,
            concat_axis=0,
            tiled=True,
        ),
        lax.all_to_all(
            run_total.reshape(sources, owned_rows, H),
            "frame",
            split_axis=0,
            concat_axis=0,
            tiled=True,
        ),
    )
    global_max = jnp.max(got_max, axis=0)
    factor = jnp.exp(got_max - global_max[None])
    norms = jnp.sum(got_total * factor, axis=0)
    sums = jnp.sum(
        got_acc.reshape(sources, owned_rows, H, HEAD_DIM) * factor[:, :, :, None], axis=0
    )
    cross = (sums / norms[:, :, None]).reshape(owned_rows, feature_width)
    cross = cross.astype(jnp.bfloat16)
    mixed = latent_full + jnp.dot(cross, w_cross_out, preferred_element_type=jnp.float32)
    normed_latent = layer_norm(mixed).astype(jnp.bfloat16)
    triple = jnp.dot(normed_latent, w_self_qkv, preferred_element_type=jnp.float32).astype(
        jnp.bfloat16
    )
    self_query = triple[:, :feature_width].reshape(owned_rows, H, HEAD_DIM)
    self_key = triple[:, feature_width : 2 * feature_width]
    self_value = triple[:, 2 * feature_width :]
    every_key, every_value = (
        lax.all_gather(self_key, "frame", axis=0, tiled=True),
        lax.all_gather(self_value, "frame", axis=0, tiled=True),
    )
    every_key = every_key.reshape(total_rows, H, HEAD_DIM)
    every_value = every_value.reshape(total_rows, H, HEAD_DIM)
    score = (
        jnp.einsum("rhe,mhe->hrm", self_query, every_key, preferred_element_type=jnp.float32)
        * scale
    )
    peak = jnp.max(score, axis=2, keepdims=True)
    expo = jnp.exp(score - peak)
    probs = (expo / jnp.sum(expo, axis=2, keepdims=True)).astype(jnp.bfloat16)
    attended = jnp.einsum("hrm,mhe->rhe", probs, every_value, preferred_element_type=jnp.float32)
    attended = attended.reshape(owned_rows, feature_width).astype(jnp.bfloat16)
    return (mixed + jnp.dot(attended, w_self_out, preferred_element_type=jnp.float32)).astype(
        jnp.bfloat16
    )


RUN = 64
PAD = 8
GROUP = 2
WIDE = 256
PAIR = 2 * HEAD_DIM
LARGE = 2.0**30
BF16 = jnp.bfloat16
F32 = jnp.float32
VMEM = pltpu.VMEM


def norm(v):
    centre = v - jnp.mean(v, axis=-1, keepdims=True)
    spread = jnp.mean(centre * centre, axis=-1, keepdims=True)
    return centre * lax.rsqrt(spread + 1e-05)


def fill_stacks(stacks, j, blocks):
    for q in range(WIDE // PAIR):
        i = j * (WIDE // PAIR) + q
        wide = stacks.shape[2] // 2
        at = 0
        for block in blocks:
            turned = block[:, q * PAIR : (q + 1) * PAIR].T
            n = turned.shape[1]
            none = jnp.zeros((HEAD_DIM, n), BF16)
            stacks[i, :HEAD_DIM, at : at + n] = turned[:HEAD_DIM]
            stacks[i, HEAD_DIM:, at : at + n] = none
            stacks[i, :HEAD_DIM, wide + at : wide + at + n] = none
            stacks[i, HEAD_DIM:, wide + at : wide + at + n] = turned[HEAD_DIM:]
            at += n


def project(normed, weights, key_at, value_at, keys, values):
    n = normed.shape[0]
    for j in range(keys.shape[1] // WIDE):
        cols = slice(j * WIDE, (j + 1) * WIDE)
        k = jnp.dot(normed, weights[:, key_at + j * WIDE : key_at + (j + 1) * WIDE], preferred_element_type=F32)
        keys[:n, cols] = k.astype(BF16)
        v = jnp.dot(normed, weights[:, value_at + j * WIDE : value_at + (j + 1) * WIDE], preferred_element_type=F32)
        values[cols, :n] = v.astype(BF16).T


def attend(n, left, stacks, keys, values, scores, probs, old, new):
    pairs, wide = stacks.shape[0], stacks.shape[2]
    half = wide // 2
    tops, totals, accs = new
    masked = left is not None
    if masked:
        valid = lax.broadcasted_iota(jnp.int32, (n, wide), 0) < left
    for i in range(pairs):
        score = jnp.dot(keys[:n, i * PAIR : (i + 1) * PAIR], stacks[i], preferred_element_type=F32)
        if masked:
            score = jnp.where(valid, score, NEG)
        scores[i, :n] = score
        top = jnp.max(score, axis=0, keepdims=True)
        tops[i : i + 1] = top if old is None else jnp.maximum(old[0][i : i + 1], top)
    for i in range(pairs):
        top = tops[i : i + 1]
        weights = jnp.exp(scores[i, :n] - top)
        if masked:
            weights = jnp.where(valid, weights, 0.0)
        total = jnp.sum(weights, axis=0, keepdims=True)
        if old is not None:
            total = total + old[1][i : i + 1] * jnp.exp(old[0][i : i + 1] - top)
        totals[i : i + 1] = total
        probs[i, :n] = weights.astype(BF16)
    for i in range(pairs):
        if old is not None:
            fade = jnp.exp(old[0][i : i + 1] - tops[i : i + 1])
        for h in range(2):
            rows = slice(i * PAIR + h * HEAD_DIM, i * PAIR + (h + 1) * HEAD_DIM)
            cols = slice(h * half, (h + 1) * half)
            part = jnp.dot(values[rows, :n], probs[i, :n, cols], preferred_element_type=F32)
            if old is not None:
                part = part + old[2][rows, :] * fade[:, cols]
            accs[rows, :] = part


def attend_lazily(n, stacks, keys, values, scores, probs, old, new):
    pairs, half = stacks.shape[0], stacks.shape[2] // 2
    tops, totals, accs = new
    old_tops, old_totals, old_accs = old
    kept_tops, kept_totals = old_tops[...], old_totals[...]
    largest = None
    for i in range(pairs):
        for h in range(2):
            cols = slice(h * half, (h + 1) * half)
            score = jnp.dot(keys[:n, i * PAIR : (i + 1) * PAIR], stacks[i][:, cols], preferred_element_type=F32)
            weights = jnp.exp(score - kept_tops[i : i + 1, cols])
            total = jnp.sum(weights, axis=0, keepdims=True)
            totals[i : i + 1, cols] = kept_totals[i : i + 1, cols] + total
            probs[i, :n, cols] = weights.astype(BF16)
            largest = total if largest is None else jnp.maximum(largest, total)
    for i in range(pairs):
        for h in range(2):
            cols = slice(h * half, (h + 1) * half)
            rows = slice(i * PAIR + h * HEAD_DIM, i * PAIR + (h + 1) * HEAD_DIM)
            out = jnp.dot(values[rows, :n], probs[i, :n, cols], preferred_element_type=F32)
            accs[rows, :] = out + old_accs[rows, :]
    tops[...] = kept_tops

    @pl.when(jnp.logical_not(jnp.max(largest) < LARGE))
    def _():
        attend(n, None, stacks, keys, values, scores, probs, (old_tops[...], old_totals[...], old_accs), new)


def tag_kernel(segment, frames, out, labels, sems):
    parts = [(frames.at[:RUN], out.at[:RUN]), (frames.at[RUN:], out.at[RUN + PAD :]), (segment, labels)]
    copies = [pltpu.make_async_copy(src, dst, sems.at[i]) for i, (src, dst) in enumerate(parts)]
    for copy in copies:
        copy.start()
    copies[2].wait()
    upper = lax.broadcasted_iota(jnp.int32, (PAD, out.shape[1]), 0) < PAD // 2
    out[RUN : RUN + PAD] = jnp.where(upper, labels[0].astype(F32), labels[RUN].astype(F32)).astype(BF16)
    copies[0].wait()
    copies[1].wait()


def queries_kernel(queries, stacks):
    scale = 1.0 / math.sqrt(HEAD_DIM)
    for j in range(queries.shape[1] // WIDE):
        block = queries[:, j * WIDE : (j + 1) * WIDE].astype(F32) * scale
        fill_stacks(stacks, j, [block.astype(BF16)])


def pick_runs(pieces, mine, picked, count):
    ids = [
        jnp.max(ref[label - label % PAD : label - label % PAD + PAD, :128][label % PAD : label % PAD + PAD // 2].astype(F32))
        for ref, spots in pieces for _, label in spots
    ]
    spots = [(ref, row) for ref, places in pieces for row, _ in places]
    count[0] = 0
    for label, (ref, row) in zip(ids, spots):
        @pl.when(label.astype(jnp.int32) == mine)
        def _(ref=ref, row=row):
            at = count[0]
            picked[at] = ref[row : row + RUN, :]
            count[0] = at + 1
    found = count[0]
    for extra in range(GROUP - 1):
        picked[found + extra] = jnp.zeros(picked.shape[1:], BF16)
    return found


def cross_groups(found, group, picked, w_kv, stacks, keys, values, scores, probs, state):
    width = state[2].shape[0]

    def one_group(g, carry):
        n = group * RUN
        frames = picked[pl.ds(g * group, group)].reshape(n, picked.shape[2])
        project(norm(frames.astype(F32)).astype(BF16), w_kv, 0, width, keys, values)
        old = (state[0][...], state[1][...], state[2])
        attend(n, (found - g * group) * RUN, stacks, keys, values, scores, probs, old, state)
        return carry

    lax.fori_loop(0, (found + group - 1) // group, one_group, 0)


def places(shape):
    if shape[0] == 2 * RUN + PAD:
        return [(0, RUN), (RUN + PAD, RUN + PAD // 2)]
    return None


def early_kernel(n_pieces, rows, *refs):
    pieces = [(ref, places(ref.shape)) for ref in refs[:n_pieces]]
    stacks, w_kv, *old = refs[n_pieces : len(refs) - 9]
    tops, totals, accs, picked, keys, values, scores, probs, count = refs[len(refs) - 9 :]
    mine = (lax.axis_index("frame") * rows) // (L // NB) + 1
    if old:
        tops[...], totals[...] = old[0][...], old[1][...]
    else:
        tops[...] = jnp.full(tops.shape, NEG, F32)
        totals[...] = jnp.zeros(totals.shape, F32)
        accs[...] = jnp.zeros(accs.shape, F32)
    found = pick_runs(pieces, mine, picked, count)
    cross_groups(found, GROUP, picked, w_kv, stacks, keys, values, scores, probs, (tops, totals, accs))


def cross_kernel(n_pieces, *refs):
    (latents, stacks, w_kv, w_out, old_tops, old_totals, _, mixed_out, normed_out, tops, totals, accs,
     picked, keys, values, scores, probs, joined, count) = refs[n_pieces:]
    rows, _ = latents.shape
    mine = (lax.axis_index("frame") * rows) // (L // NB) + 1
    pieces = []
    for at, ref in enumerate(refs[:n_pieces]):
        half = [(0, RUN)] if at % 2 == 0 else [(PAD, PAD // 2)]
        pieces.append((ref, places(ref.shape) or half))
    tops[...], totals[...] = old_tops[...], old_totals[...]
    found = pick_runs(pieces, mine, picked, count)
    cross_groups(found, GROUP, picked, w_kv, stacks, keys, values, scores, probs, (tops, totals, accs))
    finish(accs, totals, joined)
    mixed = latents[...].astype(F32) + jnp.dot(joined[...], w_out[...], preferred_element_type=F32)
    mixed_out[...] = mixed
    normed_out[...] = norm(mixed).astype(BF16)


def finish(accs, totals, joined):
    half = totals.shape[1] // 2
    for i in range(totals.shape[0]):
        parts = []
        for h in range(2):
            rows = slice(i * PAIR + h * HEAD_DIM, i * PAIR + (h + 1) * HEAD_DIM)
            parts.append(accs[rows, :] / totals[i : i + 1, h * half : (h + 1) * half])
        joined[:, i * PAIR : (i + 1) * PAIR] = jnp.concatenate(parts, axis=0).astype(BF16).T


def first_kernel(mine, other, w_qkv, stacks, tops, totals, accs, keys, values, scores, probs):
    rows, width = mine.shape
    scale = 1.0 / math.sqrt(HEAD_DIM)
    both = jnp.concatenate([mine[...], other[...]], axis=0)
    for j in range(width // WIDE):
        query = jnp.dot(both, w_qkv[:, j * WIDE : (j + 1) * WIDE], preferred_element_type=F32).astype(BF16)
        fill_stacks(stacks, j, [(query.astype(F32) * scale).astype(BF16)])
    project(mine[...], w_qkv, width, 2 * width, keys, values)
    attend(rows, None, stacks, keys, values, scores, probs, None, (tops, totals, accs))


def next_kernel(n_pieces, *refs):
    sources = refs[:n_pieces]
    (w_qkv, stacks, old_tops, old_totals, old_accs, tops, totals, accs, keys, values, scores, probs) = refs[n_pieces:]
    width = accs.shape[0]
    block = jnp.concatenate([s[...] for s in sources], axis=0)
    project(block, w_qkv, width, 2 * width, keys, values)
    old = (old_tops, old_totals, old_accs)
    attend_lazily(block.shape[0], stacks, keys, values, scores, probs, old, (tops, totals, accs))


def last_kernel(n_pieces, part, *refs):
    sources = refs[:n_pieces]
    (w_qkv, stacks, old_tops, old_totals, old_accs, tops, totals, accs, away,
     keys, values, scores, probs) = refs[n_pieces:]
    pairs, lines, rows = tops.shape[0], accs.shape[0], accs.shape[1] // 2
    width = old_accs.shape[0]
    block = jnp.concatenate([s[...] for s in sources], axis=0)
    project(block, w_qkv, width + part * lines, 2 * width + part * lines, keys, values)
    span = slice(part * pairs, (part + 1) * pairs)
    old = (old_tops.at[span], old_totals.at[span], old_accs.at[part * lines : (part + 1) * lines])
    attend_lazily(
        block.shape[0], stacks.at[span], keys, values, scores, probs, old, (tops, totals, accs)
    )
    away[:lines] = accs[:, rows:]
    for i in range(pairs):
        for h in range(2):
            there = slice(h * 2 * rows + rows, (h + 1) * 2 * rows)
            at = lines + 2 * i + h
            away[at : at + 1] = tops[i : i + 1, there]
            away[at + 2 * pairs : at + 2 * pairs + 1] = totals[i : i + 1, there]


def final_kernel(part, tops, totals, accs, far, base, w_out, out, joined, merged, sums):
    pairs, lines, rows = tops.shape[0], accs.shape[0], accs.shape[1] // 2
    for i in range(pairs):
        for h in range(2):
            at = lines + 2 * i + h
            here = slice(h * 2 * rows, h * 2 * rows + rows)
            span = slice(i * PAIR + h * HEAD_DIM, i * PAIR + (h + 1) * HEAD_DIM)
            near_top, far_top = tops[i : i + 1, here], far[at : at + 1]
            top = jnp.maximum(near_top, far_top)
            near_fade, far_fade = jnp.exp(near_top - top), jnp.exp(far_top - top)
            far_total = far[at + 2 * pairs : at + 2 * pairs + 1]
            sums[i : i + 1, h * rows : (h + 1) * rows] = totals[i : i + 1, here] * near_fade + far_total * far_fade
            merged[span] = accs[span, :rows] * near_fade + far[span] * far_fade
    finish(merged, sums, joined)
    share = jnp.dot(joined[...], w_out[part * lines : (part + 1) * lines], preferred_element_type=F32)
    out[...] = (base[...] + share).astype(out.dtype)


def on_chip(x):
    return pltpu.with_memory_space_constraint(x, VMEM)


def call(kernel, args, outs, scratch, flops, limit, aliases=None, scalars=0):
    specs = [pl.BlockSpec(memory_space=pltpu.SMEM)] * scalars
    specs += [pl.BlockSpec(memory_space=VMEM)] * (len(args) - scalars)
    return pl.pallas_call(
        kernel,
        out_shape=outs,
        in_specs=specs,
        out_specs=jax.tree.map(lambda _: pl.BlockSpec(memory_space=VMEM), outs, is_leaf=lambda o: hasattr(o, "shape")),
        scratch_shapes=scratch,
        compiler_params=pltpu.CompilerParams(vmem_limit_bytes=limit << 20),
        cost_estimate=pl.CostEstimate(flops=flops, bytes_accessed=1 << 20, transcendentals=0),
        input_output_aliases=aliases or {},
    )(*args[:scalars], *[on_chip(a) for a in args[scalars:]])


def shards_ring(frames, segment, latents, latent_queries, w_kv, w_cross_out, w_self_qkv, w_self_out):
    chips = lax.axis_size("frame") // 2
    rows, width = latents.shape
    channels = frames.shape[1]
    order = [2 * k for k in range(chips // 2)] + [2 * k + 1 for k in reversed(range(chips // 2))]
    swap = [(i, i ^ 1) for i in range(2 * chips)]
    ahead = [(2 * order[k] + c, 2 * order[(k + 1) % chips] + c) for k in range(chips) for c in range(2)]
    behind = [(there, here) for here, there in ahead]

    def cross_over(x):
        return lax.ppermute(x, "frame", swap)

    def both_ways(fore, aft):
        fore = lax.ppermute(fore, "frame", ahead)
        aft = lax.ppermute(aft, "frame", behind)
        return fore, aft

    def swapped(fore, aft):
        fore = cross_over(fore)
        aft = cross_over(aft)
        return fore, aft

    def ring(x):
        cut = x.shape[0] // 2
        red, blue = (x[:cut], x[cut:]), (x[cut:], x[:cut])
        reds, blues = [], []
        for _ in range(1, chips // 2):
            red = both_ways(*red)
            blue = both_ways(*blue)
            reds.append(list(red))
            blues.append(list(blue))
        reds.append(list(both_ways(*red)))
        return reds, blues

    def gather(tagged):
        cut = tagged.shape[0] // 2 + PAD // 2
        near, far = [[tagged]], [[cross_over(tagged)]]
        fore, aft = tagged, tagged
        for hop in range(1, chips // 2 + 1):
            if hop == chips // 2:
                fore, aft = fore[:cut], aft[-cut:]
            fore, aft = both_ways(fore, aft)
            near.append([fore, aft])
            far.append(list(swapped(fore, aft)))
        return near, far

    pairs = width // PAIR
    tagged = pl.pallas_call(
        tag_kernel,
        out_shape=VMEM((frames.shape[0] + PAD, channels), BF16),
        in_specs=[pl.BlockSpec(memory_space=pl.ANY)] * 2,
        out_specs=pl.BlockSpec(memory_space=VMEM),
        scratch_shapes=[pltpu.SMEM(segment.shape, jnp.int32), pltpu.SemaphoreType.DMA((3,))],
        compiler_params=pltpu.CompilerParams(vmem_limit_bytes=2 << 20),
        cost_estimate=pl.CostEstimate(flops=1 << 34, bytes_accessed=1 << 20, transcendentals=0),
        name="tag",
    )(*[pltpu.with_memory_space_constraint(x, pltpu.HBM) for x in (segment, frames)])
    stacks = call(queries_kernel, [latent_queries], VMEM((pairs, PAIR, 2 * rows), BF16), [], 1 << 28, 4)

    def state(queries):
        return (VMEM((pairs, 2 * queries), F32), VMEM((pairs, 2 * queries), F32), VMEM((width, queries), F32))

    def work(n, queries):
        return [
            VMEM((n, width), BF16), VMEM((width, n), BF16),
            VMEM((pairs, n, 2 * queries), F32), VMEM((pairs, n, 2 * queries), BF16),
        ]

    near, far = gather(tagged)
    late = far[-2] + near[-1] + far[-1]
    kept = []
    for soon in [near[0] + far[0] + near[1]] + [far[hop - 1] + near[hop] for hop in range(2, chips // 2)]:
        n = len(soon)
        kept = call(
            functools.partial(early_kernel, n, rows), soon + [stacks, w_kv, *kept], state(rows),
            [VMEM((2 * n + GROUP, RUN, channels), BF16), *work(GROUP * RUN, rows), pltpu.SMEM((1,), jnp.int32)],
            1 << 30, 16, {n + 2: 0, n + 3: 1, n + 4: 2} if kept else None,
        )
    n = len(late)
    mixed, normed, *_ = call(
        functools.partial(cross_kernel, n),
        late + [latents, stacks, w_kv, w_cross_out, *kept],
        (VMEM((rows, width), F32), VMEM((rows, width), BF16), *state(rows)),
        [
            VMEM((2 * n + GROUP, RUN, channels), BF16), *work(GROUP * RUN, rows),
            VMEM((rows, width), BF16), pltpu.SMEM((1,), jnp.int32),
        ],
        4 << 30, 16, {n + 4: 2, n + 5: 3, n + 6: 4},
    )
    reds, blues = ring(normed)
    arrivals = [reds[0]] + [blue + red for blue, red in zip(blues, reds[1:-1])] + [blues[-1], reds[-1]]
    stacks, *kept = call(
        first_kernel, [normed, cross_over(normed), w_self_qkv],
        (VMEM((pairs, PAIR, 4 * rows), BF16), *state(2 * rows)), work(rows, 2 * rows), 1 << 30, 16,
    )
    for sources in arrivals[:-1]:
        n = len(sources)
        keys = sum(source.shape[0] for source in sources)
        kept = call(
            functools.partial(next_kernel, n), sources + [w_self_qkv, stacks, *kept],
            state(2 * rows), work(keys, 2 * rows), n << 29, 20,
        )
    sources = arrivals[-1]
    n = len(sources)
    parts, lines = pairs // 2, width // 2
    done = []
    for part in range(2):
        *near, away = call(
            functools.partial(last_kernel, n, part), sources + [w_self_qkv, stacks, *kept],
            (
                VMEM((parts, 4 * rows), F32), VMEM((parts, 4 * rows), F32), VMEM((lines, 2 * rows), F32),
                VMEM((lines + 4 * parts, rows), F32),
            ),
            [
                VMEM((rows, lines), BF16), VMEM((lines, rows), BF16),
                VMEM((parts, rows, 4 * rows), F32), VMEM((parts, rows, 4 * rows), BF16),
            ],
            1 << 29, 16,
        )
        far = cross_over(away)
        done.append([*near, far])
    out = mixed
    for part in range(2):
        whole = jax.ShapeDtypeStruct((rows, width), BF16) if part else VMEM((rows, width), F32)
        out = call(
            functools.partial(final_kernel, part), [*done[part], out, w_self_out], whole,
            [VMEM((rows, lines), BF16), VMEM((lines, rows), F32), VMEM((parts, 2 * rows), F32)],
            1 << 29, 12,
        )
    return out


def solution(mesh):
    placed = (
        P(("rep", "frame"), None),
        P(("rep", "frame")),
        P("frame", None),
        P("frame", None),
        P(),
        P(),
        P(),
        P(),
    )
    if mesh.shape["frame"] != 16:
        return jax.shard_map(
            shards_any, mesh=mesh, in_specs=placed, out_specs=P(("rep", "frame"), None), check_vma=False
        )

    return jax.shard_map(shards_ring, mesh=mesh, in_specs=placed, out_specs=P(("rep", "frame"), None), check_vma=False)
```

```python
import functools
import math

import jax
import jax.numpy as jnp
from jax import lax
from jax.experimental import pallas as pl
from jax.experimental.pallas import tpu as pltpu
from jax.sharding import PartitionSpec as P

H = 16
HEAD_DIM = 64
L = 2048
NB = 8


NEG = -1e30


def layer_norm(inputs):
    centre = inputs - jnp.mean(inputs, axis=-1, keepdims=True)
    spread = jnp.mean(centre * centre, axis=-1, keepdims=True)
    return centre * lax.rsqrt(spread + 1e-05)


def shards_any(frames, segment, latents, latent_queries, w_kv, w_cross_out, w_self_qkv, w_self_out):
    feature_width = w_kv.shape[1] // 2
    owned_rows = latents.shape[0]
    frame_count = frames.shape[0]
    scale = 1.0 / math.sqrt(HEAD_DIM)
    block_rows = L // NB
    latent_full = latents.astype(jnp.float32)
    normed = layer_norm(frames.astype(jnp.float32)).astype(jnp.bfloat16)
    keyval = jnp.dot(normed, w_kv, preferred_element_type=jnp.float32).astype(jnp.bfloat16)
    key_heads = keyval[:, :feature_width].reshape(frame_count, H, HEAD_DIM).transpose(1, 0, 2)
    value_heads = keyval[:, feature_width:].reshape(frame_count, H, HEAD_DIM).transpose(1, 0, 2)
    total_rows = owned_rows * lax.axis_size("frame")
    piece = lax.all_gather(latent_queries, "frame", axis=0, tiled=True)
    piece_rows = piece.shape[0]
    block_ids = jnp.arange(piece_rows, dtype=jnp.int32) // block_rows + 1
    allowed = segment[None, :] == block_ids[:, None]
    query_heads = piece.reshape(piece_rows, H, HEAD_DIM).transpose(1, 0, 2)

    def one_head(item):
        query_head, key_head, value_head = item
        score = (
            jnp.einsum("re,fe->rf", query_head, key_head, preferred_element_type=jnp.float32)
            * scale
        )
        score = jnp.where(allowed, score, NEG)
        block_max = jnp.max(score, axis=1)
        weights = jnp.where(allowed, jnp.exp(score - block_max[:, None]), 0.0)
        block_total = jnp.sum(weights, axis=1)
        summed = jnp.dot(
            weights.astype(jnp.bfloat16), value_head, preferred_element_type=jnp.float32
        )
        return (block_max, block_total, summed)

    block_max, block_total, summed = lax.map(one_head, (query_heads, key_heads, value_heads))
    run_max = block_max.T
    run_total = block_total.T
    joined = summed.transpose(1, 0, 2).reshape(piece_rows, feature_width)
    run_acc = joined
    run_max, run_total, run_acc = (run_max, run_total, run_acc)
    sources = lax.axis_size("frame")
    got_acc, got_max, got_total = (
        lax.all_to_all(
            run_acc.reshape(sources, owned_rows, feature_width),
            "frame",
            split_axis=0,
            concat_axis=0,
            tiled=True,
        ),
        lax.all_to_all(
            run_max.reshape(sources, owned_rows, H),
            "frame",
            split_axis=0,
            concat_axis=0,
            tiled=True,
        ),
        lax.all_to_all(
            run_total.reshape(sources, owned_rows, H),
            "frame",
            split_axis=0,
            concat_axis=0,
            tiled=True,
        ),
    )
    global_max = jnp.max(got_max, axis=0)
    factor = jnp.exp(got_max - global_max[None])
    norms = jnp.sum(got_total * factor, axis=0)
    sums = jnp.sum(
        got_acc.reshape(sources, owned_rows, H, HEAD_DIM) * factor[:, :, :, None], axis=0
    )
    cross = (sums / norms[:, :, None]).reshape(owned_rows, feature_width)
    cross = cross.astype(jnp.bfloat16)
    mixed = latent_full + jnp.dot(cross, w_cross_out, preferred_element_type=jnp.float32)
    normed_latent = layer_norm(mixed).astype(jnp.bfloat16)
    triple = jnp.dot(normed_latent, w_self_qkv, preferred_element_type=jnp.float32).astype(
        jnp.bfloat16
    )
    self_query = triple[:, :feature_width].reshape(owned_rows, H, HEAD_DIM)
    self_key = triple[:, feature_width : 2 * feature_width]
    self_value = triple[:, 2 * feature_width :]
    every_key, every_value = (
        lax.all_gather(self_key, "frame", axis=0, tiled=True),
        lax.all_gather(self_value, "frame", axis=0, tiled=True),
    )
    every_key = every_key.reshape(total_rows, H, HEAD_DIM)
    every_value = every_value.reshape(total_rows, H, HEAD_DIM)
    score = (
        jnp.einsum("rhe,mhe->hrm", self_query, every_key, preferred_element_type=jnp.float32)
        * scale
    )
    peak = jnp.max(score, axis=2, keepdims=True)
    expo = jnp.exp(score - peak)
    probs = (expo / jnp.sum(expo, axis=2, keepdims=True)).astype(jnp.bfloat16)
    attended = jnp.einsum("hrm,mhe->rhe", probs, every_value, preferred_element_type=jnp.float32)
    attended = attended.reshape(owned_rows, feature_width).astype(jnp.bfloat16)
    return (mixed + jnp.dot(attended, w_self_out, preferred_element_type=jnp.float32)).astype(
        jnp.bfloat16
    )


RUN = 64
PAD = 8
GROUP = 2
WIDE = 256
PAIR = 2 * HEAD_DIM
LARGE = 2.0**30
BF16 = jnp.bfloat16
F32 = jnp.float32
VMEM = pltpu.VMEM


def norm(v):
    centre = v - jnp.mean(v, axis=-1, keepdims=True)
    spread = jnp.mean(centre * centre, axis=-1, keepdims=True)
    return centre * lax.rsqrt(spread + 1e-05)


def fill_stacks(stacks, j, blocks):
    for q in range(WIDE // PAIR):
        i = j * (WIDE // PAIR) + q
        wide = stacks.shape[2] // 2
        at = 0
        for block in blocks:
            turned = block[:, q * PAIR : (q + 1) * PAIR].T
            n = turned.shape[1]
            none = jnp.zeros((HEAD_DIM, n), BF16)
            stacks[i, :HEAD_DIM, at : at + n] = turned[:HEAD_DIM]
            stacks[i, HEAD_DIM:, at : at + n] = none
            stacks[i, :HEAD_DIM, wide + at : wide + at + n] = none
            stacks[i, HEAD_DIM:, wide + at : wide + at + n] = turned[HEAD_DIM:]
            at += n


def project(normed, weights, key_at, value_at, keys, values):
    n = normed.shape[0]
    for j in range(keys.shape[1] // WIDE):
        cols = slice(j * WIDE, (j + 1) * WIDE)
        k = jnp.dot(normed, weights[:, key_at + j * WIDE : key_at + (j + 1) * WIDE], preferred_element_type=F32)
        keys[:n, cols] = k.astype(BF16)
        v = jnp.dot(normed, weights[:, value_at + j * WIDE : value_at + (j + 1) * WIDE], preferred_element_type=F32)
        values[cols, :n] = v.astype(BF16).T


def attend(n, left, stacks, keys, values, scores, probs, old, new):
    pairs, wide = stacks.shape[0], stacks.shape[2]
    half = wide // 2
    tops, totals, accs = new
    found_tops, found_totals = [], []
    if left is not None:
        valid = lax.broadcasted_iota(jnp.int32, (n, wide), 0) < left
    for i in range(pairs):
        score = jnp.dot(keys[:n, i * PAIR : (i + 1) * PAIR], stacks[i], preferred_element_type=F32)
        if left is not None:
            score = jnp.where(valid, score, NEG)
        scores[i, :n] = score
        top = jnp.max(score, axis=0, keepdims=True)
        found_tops.append(top if old is None else jnp.maximum(old[0][i : i + 1], top))
    for i in range(pairs):
        weights = jnp.exp(scores[i, :n] - found_tops[i])
        found_totals.append(jnp.sum(weights, axis=0, keepdims=True))
        probs[i, :n] = weights.astype(BF16)
    for i in range(pairs):
        if old is not None:
            fade = jnp.exp(old[0][i : i + 1] - found_tops[i])
            found_totals[i] = found_totals[i] + old[1][i : i + 1] * fade
        for h in range(2):
            rows = slice(i * PAIR + h * HEAD_DIM, i * PAIR + (h + 1) * HEAD_DIM)
            cols = slice(h * half, (h + 1) * half)
            part = jnp.dot(values[rows, :n], probs[i, :n, cols], preferred_element_type=F32)
            if old is not None:
                part = part + old[2][rows, :] * fade[:, cols]
            accs[rows, :] = part
    for i in range(pairs):
        tops[i : i + 1], totals[i : i + 1] = found_tops[i], found_totals[i]


def attend_lazily(n, stacks, keys, values, scores, probs, old, new):
    pairs, half = stacks.shape[0], stacks.shape[2] // 2
    tops, totals, accs = new
    old_tops, old_totals, old_accs = old
    kept_tops, kept_totals = old_tops[...], old_totals[...]
    largest = None
    for i in range(pairs):
        for h in range(2):
            cols = slice(h * half, (h + 1) * half)
            score = jnp.dot(keys[:n, i * PAIR : (i + 1) * PAIR], stacks[i][:, cols], preferred_element_type=F32)
            weights = jnp.exp(score - kept_tops[i : i + 1, cols])
            total = jnp.sum(weights, axis=0, keepdims=True)
            totals[i : i + 1, cols] = kept_totals[i : i + 1, cols] + total
            probs[i, :n, cols] = weights.astype(BF16)
            largest = total if largest is None else jnp.maximum(largest, total)
    for i in range(pairs):
        for h in range(2):
            cols = slice(h * half, (h + 1) * half)
            rows = slice(i * PAIR + h * HEAD_DIM, i * PAIR + (h + 1) * HEAD_DIM)
            out = jnp.dot(values[rows, :n], probs[i, :n, cols], preferred_element_type=F32)
            accs[rows, :] = out + old_accs[rows, :]
    tops[...] = kept_tops

    @pl.when(jnp.logical_not(jnp.max(largest) < LARGE))
    def _():
        attend(n, None, stacks, keys, values, scores, probs, (old_tops[...], old_totals[...], old_accs), new)


def tag_kernel(segment, frames, out, labels, sems):
    parts = [(frames.at[:RUN], out.at[:RUN]), (frames.at[RUN:], out.at[RUN + PAD :]), (segment, labels)]
    copies = [pltpu.make_async_copy(src, dst, sems.at[i]) for i, (src, dst) in enumerate(parts)]
    for copy in copies:
        copy.start()
    copies[2].wait()
    upper = lax.broadcasted_iota(jnp.int32, (PAD, out.shape[1]), 0) < PAD // 2
    out[RUN : RUN + PAD] = jnp.where(upper, labels[0].astype(F32), labels[RUN].astype(F32)).astype(BF16)
    copies[0].wait()
    copies[1].wait()


def queries_kernel(queries, stacks):
    scale = 1.0 / math.sqrt(HEAD_DIM)
    for j in range(queries.shape[1] // WIDE):
        block = queries[:, j * WIDE : (j + 1) * WIDE].astype(F32) * scale
        fill_stacks(stacks, j, [block.astype(BF16)])


def pick_runs(pieces, mine, picked, count):
    ids = [
        jnp.max(ref[label - label % PAD : label - label % PAD + PAD, :128][label % PAD : label % PAD + PAD // 2].astype(F32))
        for ref, spots in pieces for _, label in spots
    ]
    spots = [(ref, row) for ref, places in pieces for row, _ in places]
    count[0] = 0
    for label, (ref, row) in zip(ids, spots):
        @pl.when(label.astype(jnp.int32) == mine)
        def _(ref=ref, row=row):
            at = count[0]
            picked[at] = ref[row : row + RUN, :]
            count[0] = at + 1
    found = count[0]
    for extra in range(GROUP - 1):
        picked[found + extra] = jnp.zeros(picked.shape[1:], BF16)
    return found


def cross_groups(found, group, picked, w_kv, stacks, keys, values, scores, probs, state):
    width = state[2].shape[0]

    def one_group(g, carry):
        n = group * RUN
        frames = picked[pl.ds(g * group, group)].reshape(n, picked.shape[2])
        project(norm(frames.astype(F32)).astype(BF16), w_kv, 0, width, keys, values)
        old = (state[0][...], state[1][...], state[2])
        attend(n, (found - g * group) * RUN, stacks, keys, values, scores, probs, old, state)
        return carry

    lax.fori_loop(0, (found + group - 1) // group, one_group, 0)


def places(shape):
    if shape[0] == 2 * RUN + PAD:
        return [(0, RUN), (RUN + PAD, RUN + PAD // 2)]
    return None


def early_kernel(n_pieces, rows, *refs):
    pieces = [(ref, places(ref.shape)) for ref in refs[:n_pieces]]
    stacks, w_kv, *old = refs[n_pieces : len(refs) - 9]
    tops, totals, accs, picked, keys, values, scores, probs, count = refs[len(refs) - 9 :]
    mine = (lax.axis_index("frame") * rows) // (L // NB) + 1
    if old:
        tops[...], totals[...] = old[0][...], old[1][...]
    else:
        tops[...] = jnp.full(tops.shape, NEG, F32)
        totals[...] = jnp.zeros(totals.shape, F32)
        accs[...] = jnp.zeros(accs.shape, F32)
    found = pick_runs(pieces, mine, picked, count)
    cross_groups(found, GROUP, picked, w_kv, stacks, keys, values, scores, probs, (tops, totals, accs))


def cross_kernel(n_pieces, *refs):
    (latents, stacks, w_kv, w_out, old_tops, old_totals, _, mixed_out, normed_out, tops, totals, accs,
     picked, keys, values, scores, probs, joined, count) = refs[n_pieces:]
    rows, _ = latents.shape
    mine = (lax.axis_index("frame") * rows) // (L // NB) + 1
    pieces = []
    for at, ref in enumerate(refs[:n_pieces]):
        half = [(0, RUN)] if at % 2 == 0 else [(PAD, PAD // 2)]
        pieces.append((ref, places(ref.shape) or half))
    tops[...], totals[...] = old_tops[...], old_totals[...]
    found = pick_runs(pieces, mine, picked, count)
    cross_groups(found, GROUP, picked, w_kv, stacks, keys, values, scores, probs, (tops, totals, accs))
    finish(accs, totals, joined)
    mixed = latents[...].astype(F32) + jnp.dot(joined[...], w_out[...], preferred_element_type=F32)
    mixed_out[...] = mixed
    normed_out[...] = norm(mixed).astype(BF16)


def finish(accs, totals, joined):
    half = totals.shape[1] // 2
    for i in range(totals.shape[0]):
        parts = []
        for h in range(2):
            rows = slice(i * PAIR + h * HEAD_DIM, i * PAIR + (h + 1) * HEAD_DIM)
            parts.append(accs[rows, :] / totals[i : i + 1, h * half : (h + 1) * half])
        joined[:, i * PAIR : (i + 1) * PAIR] = jnp.concatenate(parts, axis=0).astype(BF16).T


def first_kernel(mine, other, w_qkv, stacks, tops, totals, accs, keys, values, scores, probs):
    rows, width = mine.shape
    scale = 1.0 / math.sqrt(HEAD_DIM)
    both = jnp.concatenate([mine[...], other[...]], axis=0)
    for j in range(width // WIDE):
        query = jnp.dot(both, w_qkv[:, j * WIDE : (j + 1) * WIDE], preferred_element_type=F32).astype(BF16)
        fill_stacks(stacks, j, [(query.astype(F32) * scale).astype(BF16)])
    project(mine[...], w_qkv, width, 2 * width, keys, values)
    attend(rows, None, stacks, keys, values, scores, probs, None, (tops, totals, accs))


def next_kernel(n_pieces, *refs):
    sources = refs[:n_pieces]
    (w_qkv, stacks, old_tops, old_totals, old_accs, tops, totals, accs, keys, values, scores, probs) = refs[n_pieces:]
    width = accs.shape[0]
    block = jnp.concatenate([s[...] for s in sources], axis=0)
    project(block, w_qkv, width, 2 * width, keys, values)
    old = (old_tops, old_totals, old_accs)
    attend_lazily(block.shape[0], stacks, keys, values, scores, probs, old, (tops, totals, accs))


def export_kernel(stacks, tops, totals, accs, own_stacks, own_tops, own_totals, own_accs, away):
    pairs, width, rows = tops.shape[0], accs.shape[0], accs.shape[1] // 2
    own_accs[...] = accs[:, :rows]
    away[:width] = accs[:, rows:]
    for h in range(2):
        mine = slice(h * 2 * rows, h * 2 * rows + rows)
        cols = slice(h * rows, (h + 1) * rows)
        own_tops[:, cols] = tops[:, mine]
        own_totals[:, cols] = totals[:, mine]
        for i in range(pairs):
            own_stacks[i, :, cols] = stacks[i, :, mine]
            theirs = slice(h * 2 * rows + rows, (h + 1) * 2 * rows)
            at = width + 2 * i + h
            away[at : at + 1] = tops[i : i + 1, theirs]
            away[at + 2 * pairs : at + 2 * pairs + 1] = totals[i : i + 1, theirs]


def end_kernel(n_pieces, *refs):
    sources = refs[:n_pieces]
    (w_qkv, stacks, old_tops, old_totals, old_accs, far, mixed, w_out, out, tops, totals, accs,
     keys, values, scores, probs, joined, staged, sems) = refs[n_pieces:]
    next_kernel(n_pieces, *sources, w_qkv, stacks, old_tops, old_totals, old_accs, tops, totals, accs,
                keys, values, scores, probs)
    pairs, width, rows = tops.shape[0], accs.shape[0], accs.shape[1]
    for i in range(pairs):
        for h in range(2):
            at = width + 2 * i + h
            here = slice(h * rows, (h + 1) * rows)
            lines = slice(i * PAIR + h * HEAD_DIM, i * PAIR + (h + 1) * HEAD_DIM)
            near_top, far_top = tops[i : i + 1, here], far[at : at + 1]
            top = jnp.maximum(near_top, far_top)
            near_fade, far_fade = jnp.exp(near_top - top), jnp.exp(far_top - top)
            far_total = far[at + 2 * pairs : at + 2 * pairs + 1]
            totals[i : i + 1, here] = totals[i : i + 1, here] * near_fade + far_total * far_fade
            accs[lines] = accs[lines] * near_fade + far[lines] * far_fade
    finish(accs, totals, joined)
    copies = []
    for q in range(width // WIDE):
        cols = slice(q * WIDE, (q + 1) * WIDE)
        share = jnp.dot(joined[...], w_out[:, cols], preferred_element_type=F32)
        staged[:, cols] = (mixed[:, cols] + share).astype(BF16)
        copies.append(pltpu.make_async_copy(staged.at[:, cols], out.at[:, cols], sems.at[q]))
        copies[-1].start()
    for copy in copies:
        copy.wait()


def on_chip(x):
    return pltpu.with_memory_space_constraint(x, VMEM)


def call(kernel, args, outs, scratch, flops, limit, aliases=None, scalars=0, space=VMEM):
    specs = [pl.BlockSpec(memory_space=pltpu.SMEM)] * scalars
    specs += [pl.BlockSpec(memory_space=VMEM)] * (len(args) - scalars)
    return pl.pallas_call(
        kernel,
        out_shape=outs,
        in_specs=specs,
        out_specs=jax.tree.map(lambda _: pl.BlockSpec(memory_space=space), outs, is_leaf=lambda o: hasattr(o, "shape")),
        scratch_shapes=scratch,
        compiler_params=pltpu.CompilerParams(vmem_limit_bytes=limit << 20),
        cost_estimate=pl.CostEstimate(flops=flops, bytes_accessed=1 << 20, transcendentals=0),
        input_output_aliases=aliases or {},
    )(*args[:scalars], *[on_chip(a) for a in args[scalars:]])


def shards_ring(frames, segment, latents, latent_queries, w_kv, w_cross_out, w_self_qkv, w_self_out):
    chips = lax.axis_size("frame") // 2
    rows, width = latents.shape
    channels = frames.shape[1]
    order = [2 * k for k in range(chips // 2)] + [2 * k + 1 for k in reversed(range(chips // 2))]
    swap = [(i, i ^ 1) for i in range(2 * chips)]
    ahead = [(2 * order[k] + c, 2 * order[(k + 1) % chips] + c) for k in range(chips) for c in range(2)]
    behind = [(there, here) for here, there in ahead]

    def cross_over(x):
        return lax.ppermute(x, "frame", swap)

    def both_ways(fore, aft):
        fore = lax.ppermute(fore, "frame", ahead)
        aft = lax.ppermute(aft, "frame", behind)
        return fore, aft

    def swapped(fore, aft):
        fore = cross_over(fore)
        aft = cross_over(aft)
        return fore, aft

    def ring(x):
        cut = x.shape[0] // 2
        red, blue = (x[:cut], x[cut:]), (x[cut:], x[:cut])
        reds, blues = [], []
        for _ in range(1, chips // 2):
            red = both_ways(*red)
            blue = both_ways(*blue)
            reds.append(list(red))
            blues.append(list(blue))
        reds.append(list(both_ways(*red)))
        return reds, blues

    def gather(tagged):
        cut = tagged.shape[0] // 2 + PAD // 2
        near, far = [[tagged]], [[cross_over(tagged)]]
        fore, aft = tagged, tagged
        for hop in range(1, chips // 2 + 1):
            if hop == chips // 2:
                fore, aft = fore[:cut], aft[-cut:]
            fore, aft = both_ways(fore, aft)
            near.append([fore, aft])
            far.append(list(swapped(fore, aft)))
        return near, far

    pairs = width // PAIR
    tagged = pl.pallas_call(
        tag_kernel,
        out_shape=VMEM((frames.shape[0] + PAD, channels), BF16),
        in_specs=[pl.BlockSpec(memory_space=pl.ANY)] * 2,
        out_specs=pl.BlockSpec(memory_space=VMEM),
        scratch_shapes=[pltpu.SMEM(segment.shape, jnp.int32), pltpu.SemaphoreType.DMA((3,))],
        compiler_params=pltpu.CompilerParams(vmem_limit_bytes=2 << 20),
        cost_estimate=pl.CostEstimate(flops=1 << 34, bytes_accessed=1 << 20, transcendentals=0),
        name="tag",
    )(*[pltpu.with_memory_space_constraint(x, pltpu.HBM) for x in (segment, frames)])
    stacks = call(queries_kernel, [latent_queries], VMEM((pairs, PAIR, 2 * rows), BF16), [], 1 << 28, 4)

    def state(queries):
        return (VMEM((pairs, 2 * queries), F32), VMEM((pairs, 2 * queries), F32), VMEM((width, queries), F32))

    def work(n, queries):
        return [
            VMEM((n, width), BF16), VMEM((width, n), BF16),
            VMEM((pairs, n, 2 * queries), F32), VMEM((pairs, n, 2 * queries), BF16),
        ]

    near, far = gather(tagged)
    late = far[-2] + near[-1] + far[-1]
    kept = []
    for soon in [near[0] + far[0] + near[1]] + [far[hop - 1] + near[hop] for hop in range(2, chips // 2)]:
        n = len(soon)
        kept = call(
            functools.partial(early_kernel, n, rows), soon + [stacks, w_kv, *kept], state(rows),
            [VMEM((2 * n + GROUP, RUN, channels), BF16), *work(GROUP * RUN, rows), pltpu.SMEM((1,), jnp.int32)],
            1 << 30, 16, {n + 2: 0, n + 3: 1, n + 4: 2} if kept else None,
        )
    n = len(late)
    mixed, normed, *_ = call(
        functools.partial(cross_kernel, n),
        late + [latents, stacks, w_kv, w_cross_out, *kept],
        (VMEM((rows, width), F32), VMEM((rows, width), BF16), *state(rows)),
        [
            VMEM((2 * n + GROUP, RUN, channels), BF16), *work(GROUP * RUN, rows),
            VMEM((rows, width), BF16), pltpu.SMEM((1,), jnp.int32),
        ],
        4 << 30, 16, {n + 4: 2, n + 5: 3, n + 6: 4},
    )
    reds, blues = ring(normed)
    arrivals = [reds[0]] + [blue + red for blue, red in zip(blues, reds[1:-1])] + [blues[-1], reds[-1]]
    stacks, *kept = call(
        first_kernel, [normed, cross_over(normed), w_self_qkv],
        (VMEM((pairs, PAIR, 4 * rows), BF16), *state(2 * rows)), work(rows, 2 * rows), 1 << 30, 16,
    )
    for sources in arrivals[:-1]:
        n = len(sources)
        keys = sum(source.shape[0] for source in sources)
        kept = call(
            functools.partial(next_kernel, n), sources + [w_self_qkv, stacks, *kept],
            state(2 * rows), work(keys, 2 * rows), n << 29, 20,
        )
    own_stacks, *own, away = call(
        export_kernel, [stacks, *kept],
        (VMEM((pairs, PAIR, 2 * rows), BF16), *state(rows), VMEM((width + 4 * pairs, rows), F32)),
        [], 1 << 20, 8,
    )
    far = cross_over(away)
    sources = arrivals[-1]
    others = swapped(*sources)
    own = call(
        functools.partial(next_kernel, 2), [*sources, w_self_qkv, own_stacks, *own],
        state(rows), work(rows, rows), 1 << 29, 16,
    )
    return call(
        functools.partial(end_kernel, 2),
        [*others, w_self_qkv, own_stacks, *own, far, mixed, w_self_out],
        jax.ShapeDtypeStruct((rows, width), BF16),
        [
            *state(rows), *work(rows, rows), VMEM((rows, width), BF16), VMEM((rows, width), BF16),
            pltpu.SemaphoreType.DMA((width // WIDE,)),
        ],
        1 << 30, 16, space=pl.ANY,
    )


def solution(mesh):
    placed = (
        P(("rep", "frame"), None),
        P(("rep", "frame")),
        P("frame", None),
        P("frame", None),
        P(),
        P(),
        P(),
        P(),
    )
    if mesh.shape["frame"] != 16:
        return jax.shard_map(
            shards_any, mesh=mesh, in_specs=placed, out_specs=P(("rep", "frame"), None), check_vma=False
        )

    return jax.shard_map(shards_ring, mesh=mesh, in_specs=placed, out_specs=P(("rep", "frame"), None), check_vma=False)
```

```python
import functools
import math

import jax
import jax.numpy as jnp
from jax import lax
from jax.experimental import pallas as pl
from jax.experimental.pallas import tpu as pltpu
from jax.sharding import PartitionSpec as P

H = 16
HEAD_DIM = 64
L = 2048
NB = 8


NEG = -1e30


def layer_norm(inputs):
    centre = inputs - jnp.mean(inputs, axis=-1, keepdims=True)
    spread = jnp.mean(centre * centre, axis=-1, keepdims=True)
    return centre * lax.rsqrt(spread + 1e-05)


def shards_any(frames, segment, latents, latent_queries, w_kv, w_cross_out, w_self_qkv, w_self_out):
    feature_width = w_kv.shape[1] // 2
    owned_rows = latents.shape[0]
    frame_count = frames.shape[0]
    scale = 1.0 / math.sqrt(HEAD_DIM)
    block_rows = L // NB
    latent_full = latents.astype(jnp.float32)
    normed = layer_norm(frames.astype(jnp.float32)).astype(jnp.bfloat16)
    keyval = jnp.dot(normed, w_kv, preferred_element_type=jnp.float32).astype(jnp.bfloat16)
    key_heads = keyval[:, :feature_width].reshape(frame_count, H, HEAD_DIM).transpose(1, 0, 2)
    value_heads = keyval[:, feature_width:].reshape(frame_count, H, HEAD_DIM).transpose(1, 0, 2)
    total_rows = owned_rows * lax.axis_size("frame")
    piece = lax.all_gather(latent_queries, "frame", axis=0, tiled=True)
    piece_rows = piece.shape[0]
    block_ids = jnp.arange(piece_rows, dtype=jnp.int32) // block_rows + 1
    allowed = segment[None, :] == block_ids[:, None]
    query_heads = piece.reshape(piece_rows, H, HEAD_DIM).transpose(1, 0, 2)

    def one_head(item):
        query_head, key_head, value_head = item
        score = (
            jnp.einsum("re,fe->rf", query_head, key_head, preferred_element_type=jnp.float32)
            * scale
        )
        score = jnp.where(allowed, score, NEG)
        block_max = jnp.max(score, axis=1)
        weights = jnp.where(allowed, jnp.exp(score - block_max[:, None]), 0.0)
        block_total = jnp.sum(weights, axis=1)
        summed = jnp.dot(
            weights.astype(jnp.bfloat16), value_head, preferred_element_type=jnp.float32
        )
        return (block_max, block_total, summed)

    block_max, block_total, summed = lax.map(one_head, (query_heads, key_heads, value_heads))
    run_max = block_max.T
    run_total = block_total.T
    joined = summed.transpose(1, 0, 2).reshape(piece_rows, feature_width)
    run_acc = joined
    run_max, run_total, run_acc = (run_max, run_total, run_acc)
    sources = lax.axis_size("frame")
    got_acc, got_max, got_total = (
        lax.all_to_all(
            run_acc.reshape(sources, owned_rows, feature_width),
            "frame",
            split_axis=0,
            concat_axis=0,
            tiled=True,
        ),
        lax.all_to_all(
            run_max.reshape(sources, owned_rows, H),
            "frame",
            split_axis=0,
            concat_axis=0,
            tiled=True,
        ),
        lax.all_to_all(
            run_total.reshape(sources, owned_rows, H),
            "frame",
            split_axis=0,
            concat_axis=0,
            tiled=True,
        ),
    )
    global_max = jnp.max(got_max, axis=0)
    factor = jnp.exp(got_max - global_max[None])
    norms = jnp.sum(got_total * factor, axis=0)
    sums = jnp.sum(
        got_acc.reshape(sources, owned_rows, H, HEAD_DIM) * factor[:, :, :, None], axis=0
    )
    cross = (sums / norms[:, :, None]).reshape(owned_rows, feature_width)
    cross = cross.astype(jnp.bfloat16)
    mixed = latent_full + jnp.dot(cross, w_cross_out, preferred_element_type=jnp.float32)
    normed_latent = layer_norm(mixed).astype(jnp.bfloat16)
    triple = jnp.dot(normed_latent, w_self_qkv, preferred_element_type=jnp.float32).astype(
        jnp.bfloat16
    )
    self_query = triple[:, :feature_width].reshape(owned_rows, H, HEAD_DIM)
    self_key = triple[:, feature_width : 2 * feature_width]
    self_value = triple[:, 2 * feature_width :]
    every_key, every_value = (
        lax.all_gather(self_key, "frame", axis=0, tiled=True),
        lax.all_gather(self_value, "frame", axis=0, tiled=True),
    )
    every_key = every_key.reshape(total_rows, H, HEAD_DIM)
    every_value = every_value.reshape(total_rows, H, HEAD_DIM)
    score = (
        jnp.einsum("rhe,mhe->hrm", self_query, every_key, preferred_element_type=jnp.float32)
        * scale
    )
    peak = jnp.max(score, axis=2, keepdims=True)
    expo = jnp.exp(score - peak)
    probs = (expo / jnp.sum(expo, axis=2, keepdims=True)).astype(jnp.bfloat16)
    attended = jnp.einsum("hrm,mhe->rhe", probs, every_value, preferred_element_type=jnp.float32)
    attended = attended.reshape(owned_rows, feature_width).astype(jnp.bfloat16)
    return (mixed + jnp.dot(attended, w_self_out, preferred_element_type=jnp.float32)).astype(
        jnp.bfloat16
    )


RUN = 64
PAD = 8
GROUP = 2
WIDE = 256
PAIR = 2 * HEAD_DIM
LARGE = 2.0**30
BF16 = jnp.bfloat16
F32 = jnp.float32
VMEM = pltpu.VMEM


def norm(v):
    centre = v - jnp.mean(v, axis=-1, keepdims=True)
    spread = jnp.mean(centre * centre, axis=-1, keepdims=True)
    return centre * lax.rsqrt(spread + 1e-05)


def fill_stacks(stacks, j, blocks):
    for q in range(WIDE // PAIR):
        i = j * (WIDE // PAIR) + q
        wide = stacks.shape[2] // 2
        at = 0
        for block in blocks:
            turned = block[:, q * PAIR : (q + 1) * PAIR].T
            n = turned.shape[1]
            none = jnp.zeros((HEAD_DIM, n), BF16)
            stacks[i, :HEAD_DIM, at : at + n] = turned[:HEAD_DIM]
            stacks[i, HEAD_DIM:, at : at + n] = none
            stacks[i, :HEAD_DIM, wide + at : wide + at + n] = none
            stacks[i, HEAD_DIM:, wide + at : wide + at + n] = turned[HEAD_DIM:]
            at += n


def project(normed, weights, key_at, value_at, keys, values):
    n = normed.shape[0]
    for j in range(keys.shape[1] // WIDE):
        cols = slice(j * WIDE, (j + 1) * WIDE)
        k = jnp.dot(normed, weights[:, key_at + j * WIDE : key_at + (j + 1) * WIDE], preferred_element_type=F32)
        keys[:n, cols] = k.astype(BF16)
        v = jnp.dot(normed, weights[:, value_at + j * WIDE : value_at + (j + 1) * WIDE], preferred_element_type=F32)
        values[cols, :n] = v.astype(BF16).T


def attend(n, left, stacks, keys, values, scores, probs, old, new):
    pairs, wide = stacks.shape[0], stacks.shape[2]
    half = wide // 2
    tops, totals, accs = new
    found_tops, found_totals = [], []
    if left is not None:
        valid = lax.broadcasted_iota(jnp.int32, (n, wide), 0) < left
    for i in range(pairs):
        score = jnp.dot(keys[:n, i * PAIR : (i + 1) * PAIR], stacks[i], preferred_element_type=F32)
        if left is not None:
            score = jnp.where(valid, score, NEG)
        scores[i, :n] = score
        top = jnp.max(score, axis=0, keepdims=True)
        found_tops.append(top if old is None else jnp.maximum(old[0][i : i + 1], top))
    for i in range(pairs):
        weights = jnp.exp(scores[i, :n] - found_tops[i])
        found_totals.append(jnp.sum(weights, axis=0, keepdims=True))
        probs[i, :n] = weights.astype(BF16)
    for i in range(pairs):
        if old is not None:
            fade = jnp.exp(old[0][i : i + 1] - found_tops[i])
            found_totals[i] = found_totals[i] + old[1][i : i + 1] * fade
        for h in range(2):
            rows = slice(i * PAIR + h * HEAD_DIM, i * PAIR + (h + 1) * HEAD_DIM)
            cols = slice(h * half, (h + 1) * half)
            part = jnp.dot(values[rows, :n], probs[i, :n, cols], preferred_element_type=F32)
            if old is not None:
                part = part + old[2][rows, :] * fade[:, cols]
            accs[rows, :] = part
    for i in range(pairs):
        tops[i : i + 1], totals[i : i + 1] = found_tops[i], found_totals[i]


def attend_lazily(n, stacks, keys, values, scores, probs, old, new):
    pairs, half = stacks.shape[0], stacks.shape[2] // 2
    tops, totals, accs = new
    old_tops, old_totals, old_accs = old
    kept_tops, kept_totals = old_tops[...], old_totals[...]
    largest = None
    for i in range(pairs):
        for h in range(2):
            cols = slice(h * half, (h + 1) * half)
            score = jnp.dot(keys[:n, i * PAIR : (i + 1) * PAIR], stacks[i][:, cols], preferred_element_type=F32)
            weights = jnp.exp(score - kept_tops[i : i + 1, cols])
            total = jnp.sum(weights, axis=0, keepdims=True)
            totals[i : i + 1, cols] = kept_totals[i : i + 1, cols] + total
            probs[i, :n, cols] = weights.astype(BF16)
            largest = total if largest is None else jnp.maximum(largest, total)
    for i in range(pairs):
        for h in range(2):
            cols = slice(h * half, (h + 1) * half)
            rows = slice(i * PAIR + h * HEAD_DIM, i * PAIR + (h + 1) * HEAD_DIM)
            out = jnp.dot(values[rows, :n], probs[i, :n, cols], preferred_element_type=F32)
            accs[rows, :] = out + old_accs[rows, :]
    tops[...] = kept_tops

    @pl.when(jnp.logical_not(jnp.max(largest) < LARGE))
    def _():
        attend(n, None, stacks, keys, values, scores, probs, (old_tops[...], old_totals[...], old_accs), new)


def tag_kernel(segment, frames, out, labels, sems):
    parts = [(frames.at[:RUN], out.at[:RUN]), (frames.at[RUN:], out.at[RUN + PAD :]), (segment, labels)]
    copies = [pltpu.make_async_copy(src, dst, sems.at[i]) for i, (src, dst) in enumerate(parts)]
    for copy in copies:
        copy.start()
    copies[2].wait()
    upper = lax.broadcasted_iota(jnp.int32, (PAD, out.shape[1]), 0) < PAD // 2
    out[RUN : RUN + PAD] = jnp.where(upper, labels[0].astype(F32), labels[RUN].astype(F32)).astype(BF16)
    copies[0].wait()
    copies[1].wait()


def queries_kernel(queries, stacks):
    scale = 1.0 / math.sqrt(HEAD_DIM)
    for j in range(queries.shape[1] // WIDE):
        block = queries[:, j * WIDE : (j + 1) * WIDE].astype(F32) * scale
        fill_stacks(stacks, j, [block.astype(BF16)])


def pick_runs(pieces, mine, picked, count):
    ids = [
        jnp.max(ref[label - label % PAD : label - label % PAD + PAD, :128][label % PAD : label % PAD + PAD // 2].astype(F32))
        for ref, spots in pieces for _, label in spots
    ]
    spots = [(ref, row) for ref, places in pieces for row, _ in places]
    count[0] = 0
    for label, (ref, row) in zip(ids, spots):
        @pl.when(label.astype(jnp.int32) == mine)
        def _(ref=ref, row=row):
            at = count[0]
            picked[at] = ref[row : row + RUN, :]
            count[0] = at + 1
    found = count[0]
    for extra in range(GROUP - 1):
        picked[found + extra] = jnp.zeros(picked.shape[1:], BF16)
    return found


def cross_groups(found, group, picked, w_kv, stacks, keys, values, scores, probs, state):
    width = state[2].shape[0]

    def one_group(g, carry):
        n = group * RUN
        frames = picked[pl.ds(g * group, group)].reshape(n, picked.shape[2])
        project(norm(frames.astype(F32)).astype(BF16), w_kv, 0, width, keys, values)
        old = (state[0][...], state[1][...], state[2])
        attend(n, (found - g * group) * RUN, stacks, keys, values, scores, probs, old, state)
        return carry

    lax.fori_loop(0, (found + group - 1) // group, one_group, 0)


def places(shape):
    if shape[0] == 2 * RUN + PAD:
        return [(0, RUN), (RUN + PAD, RUN + PAD // 2)]
    return None


def early_kernel(n_pieces, rows, *refs):
    pieces = [(ref, places(ref.shape)) for ref in refs[:n_pieces]]
    stacks, w_kv, *old = refs[n_pieces : len(refs) - 9]
    tops, totals, accs, picked, keys, values, scores, probs, count = refs[len(refs) - 9 :]
    mine = (lax.axis_index("frame") * rows) // (L // NB) + 1
    if old:
        tops[...], totals[...] = old[0][...], old[1][...]
    else:
        tops[...] = jnp.full(tops.shape, NEG, F32)
        totals[...] = jnp.zeros(totals.shape, F32)
        accs[...] = jnp.zeros(accs.shape, F32)
    found = pick_runs(pieces, mine, picked, count)
    cross_groups(found, GROUP, picked, w_kv, stacks, keys, values, scores, probs, (tops, totals, accs))


def cross_kernel(n_pieces, *refs):
    (latents, stacks, w_kv, w_out, old_tops, old_totals, _, mixed_out, normed_out, tops, totals, accs,
     picked, keys, values, scores, probs, joined, count) = refs[n_pieces:]
    rows, _ = latents.shape
    mine = (lax.axis_index("frame") * rows) // (L // NB) + 1
    pieces = []
    for at, ref in enumerate(refs[:n_pieces]):
        half = [(0, RUN)] if at % 2 == 0 else [(PAD, PAD // 2)]
        pieces.append((ref, places(ref.shape) or half))
    tops[...], totals[...] = old_tops[...], old_totals[...]
    found = pick_runs(pieces, mine, picked, count)
    cross_groups(found, GROUP, picked, w_kv, stacks, keys, values, scores, probs, (tops, totals, accs))
    finish(accs, totals, joined)
    mixed = latents[...].astype(F32) + jnp.dot(joined[...], w_out[...], preferred_element_type=F32)
    mixed_out[...] = mixed
    normed_out[...] = norm(mixed).astype(BF16)


def finish(accs, totals, joined):
    half = totals.shape[1] // 2
    for i in range(totals.shape[0]):
        parts = []
        for h in range(2):
            rows = slice(i * PAIR + h * HEAD_DIM, i * PAIR + (h + 1) * HEAD_DIM)
            parts.append(accs[rows, :] / totals[i : i + 1, h * half : (h + 1) * half])
        joined[:, i * PAIR : (i + 1) * PAIR] = jnp.concatenate(parts, axis=0).astype(BF16).T


def first_kernel(mine, other, w_qkv, stacks, tops, totals, accs, keys, values, scores, probs):
    rows, width = mine.shape
    scale = 1.0 / math.sqrt(HEAD_DIM)
    both = jnp.concatenate([mine[...], other[...]], axis=0)
    for j in range(width // WIDE):
        query = jnp.dot(both, w_qkv[:, j * WIDE : (j + 1) * WIDE], preferred_element_type=F32).astype(BF16)
        fill_stacks(stacks, j, [(query.astype(F32) * scale).astype(BF16)])
    project(mine[...], w_qkv, width, 2 * width, keys, values)
    attend(rows, None, stacks, keys, values, scores, probs, None, (tops, totals, accs))


def next_kernel(n_pieces, *refs):
    sources = refs[:n_pieces]
    (w_qkv, stacks, old_tops, old_totals, old_accs, tops, totals, accs, keys, values, scores, probs) = refs[n_pieces:]
    width = accs.shape[0]
    block = jnp.concatenate([s[...] for s in sources], axis=0)
    project(block, w_qkv, width, 2 * width, keys, values)
    old = (old_tops, old_totals, old_accs)
    attend_lazily(block.shape[0], stacks, keys, values, scores, probs, old, (tops, totals, accs))


def last_kernel(n_pieces, part, *refs):
    sources = refs[:n_pieces]
    (w_qkv, stacks, old_tops, old_totals, old_accs, tops, totals, accs, away,
     keys, values, scores, probs) = refs[n_pieces:]
    pairs, lines, rows = tops.shape[0], accs.shape[0], accs.shape[1] // 2
    width = old_accs.shape[0]
    block = jnp.concatenate([s[...] for s in sources], axis=0)
    project(block, w_qkv, width + part * lines, 2 * width + part * lines, keys, values)
    span = slice(part * pairs, (part + 1) * pairs)
    old = (old_tops.at[span], old_totals.at[span], old_accs.at[part * lines : (part + 1) * lines])
    attend_lazily(
        block.shape[0], stacks.at[span], keys, values, scores, probs, old, (tops, totals, accs)
    )
    away[:lines] = accs[:, rows:]
    for i in range(pairs):
        for h in range(2):
            there = slice(h * 2 * rows + rows, (h + 1) * 2 * rows)
            at = lines + 2 * i + h
            away[at : at + 1] = tops[i : i + 1, there]
            away[at + 2 * pairs : at + 2 * pairs + 1] = totals[i : i + 1, there]


def final_kernel(part, tops, totals, accs, far, base, w_out, out, joined, merged, sums, *rest):
    pairs, lines, rows = tops.shape[0], accs.shape[0], accs.shape[1] // 2
    for i in range(pairs):
        for h in range(2):
            at = lines + 2 * i + h
            here = slice(h * 2 * rows, h * 2 * rows + rows)
            span = slice(i * PAIR + h * HEAD_DIM, i * PAIR + (h + 1) * HEAD_DIM)
            near_top, far_top = tops[i : i + 1, here], far[at : at + 1]
            top = jnp.maximum(near_top, far_top)
            near_fade, far_fade = jnp.exp(near_top - top), jnp.exp(far_top - top)
            far_total = far[at + 2 * pairs : at + 2 * pairs + 1]
            sums[i : i + 1, h * rows : (h + 1) * rows] = totals[i : i + 1, here] * near_fade + far_total * far_fade
            merged[span] = accs[span, :rows] * near_fade + far[span] * far_fade
    finish(merged, sums, joined)
    copies = []
    for q in range(out.shape[1] // WIDE):
        cols = slice(q * WIDE, (q + 1) * WIDE)
        share = jnp.dot(joined[...], w_out[part * lines : (part + 1) * lines, cols], preferred_element_type=F32)
        if not rest:
            out[:, cols] = base[:, cols] + share
            continue
        staged, sems = rest
        staged[:, cols] = (base[:, cols] + share).astype(BF16)
        copies.append(pltpu.make_async_copy(staged.at[:, cols], out.at[:, cols], sems.at[q]))
        copies[-1].start()
    for copy in copies:
        copy.wait()


def on_chip(x):
    return pltpu.with_memory_space_constraint(x, VMEM)


def call(kernel, args, outs, scratch, flops, limit, aliases=None, scalars=0, space=VMEM):
    specs = [pl.BlockSpec(memory_space=pltpu.SMEM)] * scalars
    specs += [pl.BlockSpec(memory_space=VMEM)] * (len(args) - scalars)
    return pl.pallas_call(
        kernel,
        out_shape=outs,
        in_specs=specs,
        out_specs=jax.tree.map(lambda _: pl.BlockSpec(memory_space=space), outs, is_leaf=lambda o: hasattr(o, "shape")),
        scratch_shapes=scratch,
        compiler_params=pltpu.CompilerParams(vmem_limit_bytes=limit << 20),
        cost_estimate=pl.CostEstimate(flops=flops, bytes_accessed=1 << 20, transcendentals=0),
        input_output_aliases=aliases or {},
    )(*args[:scalars], *[on_chip(a) for a in args[scalars:]])


def shards_ring(frames, segment, latents, latent_queries, w_kv, w_cross_out, w_self_qkv, w_self_out):
    chips = lax.axis_size("frame") // 2
    rows, width = latents.shape
    channels = frames.shape[1]
    order = [2 * k for k in range(chips // 2)] + [2 * k + 1 for k in reversed(range(chips // 2))]
    swap = [(i, i ^ 1) for i in range(2 * chips)]
    ahead = [(2 * order[k] + c, 2 * order[(k + 1) % chips] + c) for k in range(chips) for c in range(2)]
    behind = [(there, here) for here, there in ahead]

    def cross_over(x):
        return lax.ppermute(x, "frame", swap)

    def both_ways(fore, aft):
        fore = lax.ppermute(fore, "frame", ahead)
        aft = lax.ppermute(aft, "frame", behind)
        return fore, aft

    def swapped(fore, aft):
        fore = cross_over(fore)
        aft = cross_over(aft)
        return fore, aft

    def ring(x):
        cut = x.shape[0] // 2
        red, blue = (x[:cut], x[cut:]), (x[cut:], x[:cut])
        reds, blues = [], []
        for _ in range(1, chips // 2):
            red = both_ways(*red)
            blue = both_ways(*blue)
            reds.append(list(red))
            blues.append(list(blue))
        reds.append(list(both_ways(*red)))
        return reds, blues

    def gather(tagged):
        cut = tagged.shape[0] // 2 + PAD // 2
        near, far = [[tagged]], [[cross_over(tagged)]]
        fore, aft = tagged, tagged
        for hop in range(1, chips // 2 + 1):
            if hop == chips // 2:
                fore, aft = fore[:cut], aft[-cut:]
            fore, aft = both_ways(fore, aft)
            near.append([fore, aft])
            far.append(list(swapped(fore, aft)))
        return near, far

    pairs = width // PAIR
    tagged = pl.pallas_call(
        tag_kernel,
        out_shape=VMEM((frames.shape[0] + PAD, channels), BF16),
        in_specs=[pl.BlockSpec(memory_space=pl.ANY)] * 2,
        out_specs=pl.BlockSpec(memory_space=VMEM),
        scratch_shapes=[pltpu.SMEM(segment.shape, jnp.int32), pltpu.SemaphoreType.DMA((3,))],
        compiler_params=pltpu.CompilerParams(vmem_limit_bytes=2 << 20),
        cost_estimate=pl.CostEstimate(flops=1 << 34, bytes_accessed=1 << 20, transcendentals=0),
        name="tag",
    )(*[pltpu.with_memory_space_constraint(x, pltpu.HBM) for x in (segment, frames)])
    stacks = call(queries_kernel, [latent_queries], VMEM((pairs, PAIR, 2 * rows), BF16), [], 1 << 28, 4)

    def state(queries):
        return (VMEM((pairs, 2 * queries), F32), VMEM((pairs, 2 * queries), F32), VMEM((width, queries), F32))

    def work(n, queries):
        return [
            VMEM((n, width), BF16), VMEM((width, n), BF16),
            VMEM((pairs, n, 2 * queries), F32), VMEM((pairs, n, 2 * queries), BF16),
        ]

    near, far = gather(tagged)
    late = far[-2] + near[-1] + far[-1]
    kept = []
    for soon in [near[0] + far[0] + near[1]] + [far[hop - 1] + near[hop] for hop in range(2, chips // 2)]:
        n = len(soon)
        kept = call(
            functools.partial(early_kernel, n, rows), soon + [stacks, w_kv, *kept], state(rows),
            [VMEM((2 * n + GROUP, RUN, channels), BF16), *work(GROUP * RUN, rows), pltpu.SMEM((1,), jnp.int32)],
            1 << 30, 16, {n + 2: 0, n + 3: 1, n + 4: 2} if kept else None,
        )
    n = len(late)
    mixed, normed, *_ = call(
        functools.partial(cross_kernel, n),
        late + [latents, stacks, w_kv, w_cross_out, *kept],
        (VMEM((rows, width), F32), VMEM((rows, width), BF16), *state(rows)),
        [
            VMEM((2 * n + GROUP, RUN, channels), BF16), *work(GROUP * RUN, rows),
            VMEM((rows, width), BF16), pltpu.SMEM((1,), jnp.int32),
        ],
        4 << 30, 16, {n + 4: 2, n + 5: 3, n + 6: 4},
    )
    reds, blues = ring(normed)
    arrivals = [reds[0]] + [blue + red for blue, red in zip(blues, reds[1:-1])] + [blues[-1], reds[-1]]
    stacks, *kept = call(
        first_kernel, [normed, cross_over(normed), w_self_qkv],
        (VMEM((pairs, PAIR, 4 * rows), BF16), *state(2 * rows)), work(rows, 2 * rows), 1 << 30, 16,
    )
    for sources in arrivals[:-1]:
        n = len(sources)
        keys = sum(source.shape[0] for source in sources)
        kept = call(
            functools.partial(next_kernel, n), sources + [w_self_qkv, stacks, *kept],
            state(2 * rows), work(keys, 2 * rows), n << 29, 20,
        )
    sources = arrivals[-1]
    n = len(sources)
    parts, lines = pairs // 2, width // 2
    done = []
    for part in range(2):
        *near, away = call(
            functools.partial(last_kernel, n, part), sources + [w_self_qkv, stacks, *kept],
            (
                VMEM((parts, 4 * rows), F32), VMEM((parts, 4 * rows), F32), VMEM((lines, 2 * rows), F32),
                VMEM((lines + 4 * parts, rows), F32),
            ),
            [
                VMEM((rows, lines), BF16), VMEM((lines, rows), BF16),
                VMEM((parts, rows, 4 * rows), F32), VMEM((parts, rows, 4 * rows), BF16),
            ],
            1 << 29, 16,
        )
        far = cross_over(away)
        done.append([*near, far])
    out = mixed
    for part in range(2):
        whole = jax.ShapeDtypeStruct((rows, width), BF16) if part else VMEM((rows, width), F32)
        out = call(
            functools.partial(final_kernel, part), [*done[part], out, w_self_out], whole,
            [VMEM((rows, lines), BF16), VMEM((lines, rows), F32), VMEM((parts, 2 * rows), F32)]
            + ([VMEM((rows, width), BF16), pltpu.SemaphoreType.DMA((width // WIDE,))] if part else []),
            1 << 29, 12, space=pl.ANY if part else VMEM,
        )
    return out


def solution(mesh):
    placed = (
        P(("rep", "frame"), None),
        P(("rep", "frame")),
        P("frame", None),
        P("frame", None),
        P(),
        P(),
        P(),
        P(),
    )
    if mesh.shape["frame"] != 16:
        return jax.shard_map(
            shards_any, mesh=mesh, in_specs=placed, out_specs=P(("rep", "frame"), None), check_vma=False
        )

    return jax.shard_map(shards_ring, mesh=mesh, in_specs=placed, out_specs=P(("rep", "frame"), None), check_vma=False)
```
